32 devices in a mesh: section: 2 (over core), seq: 4 (over z), chan: 4 (over y, x).
Axes of the slice: x: 2, y: 2, z: 4, core: 2. Of those that a mesh axis runs over, the one named last changes fastest.
Arguments:
- inputs: bfloat16 [2, 256, 4096], P(None, 'seq', 'chan'), may hold values from -8 to 8
- out_grad: bfloat16 [2, 256, 4096], P(None, 'seq', 'chan'), may hold values from -0.625 to 0.625
- short_filters: float32 [2, 3, 7, 4096], P('section', None, None, 'chan'), may hold values from -2 to 2
- long_filters: float32 [2, 128, 4096], P('section', None, 'chan'), may hold values from -0.5 to 0.5
- skip_gain: float32 [2, 4096], P('section', 'chan'), may hold values from -1 to 1
- norm_gain: float32 [2, 4096], P('section', 'chan'), may hold values from 0.5 to 1.5
Outputs:
- param_grads: float32 [2, 151, 4096], P('section', None, 'chan')
The draws below stay inside these ranges and needn't reach their ends.
All inputs are finite; a program needn't handle non-finite values.
Results may differ from the reference program's by a relative error of at most 0.012.
The reference program's roundings to bfloat16 on the way count: a program that leaves them out, or rounds other values in their place, can miss the bound.
Values may be sent and summed in bfloat16 or wider, within the bound.
A program may use at most 64 MiB of HBM per device.

```python
import math
import jax
import jax.numpy as jnp
from jax import lax

D = 4096
KS = 7
KL = 128
MICRO = 2
LAYERS = 2
SEQ = 256


def draw_inputs(key, part):
    keys = jax.random.split(key, 3)
    columns = jnp.exp(jax.random.uniform(keys[1], (D,), jnp.float32, math.log(0.3), math.log(3.0)))
    base = jax.random.normal(keys[0], (MICRO, SEQ, D), jnp.float32)
    row_scales = jnp.exp(jax.random.uniform(keys[2], (MICRO, SEQ, 1), jnp.float32, math.log(0.5), math.log(2.0)))
    values = base * row_scales * columns
    return jnp.clip(values, -8.0, 8.0).astype(jnp.bfloat16)


def shard_levels(rng, extent, cuts, low, largest):
    factor_of = 1.0
    for axis_at, parts in cuts:
        heights = jax.random.uniform(jax.random.fold_in(jax.random.fold_in(rng, 6), axis_at), (parts,), jnp.float32, low / len(cuts), largest / len(cuts))
        factor_of = factor_of * jnp.repeat(jnp.exp(heights), extent[axis_at] // parts).reshape((-1,) + (1,) * (len(extent) - 1 - axis_at))
    return factor_of


def gaussian(rng, shape, scale, reach, cuts=(), held_as=jnp.bfloat16):
    array = scale * jax.random.normal(rng, shape, jnp.float32)
    if cuts:
        array = array * shard_levels(rng, shape, cuts, -0.22, 0.18)
    return jnp.clip(array, -reach, reach).astype(held_as)


def setup_inputs(seed: int = 0) -> dict:
    arg_keys = jax.random.split(jax.random.key(seed), 7)
    inputs = draw_inputs(jax.random.fold_in(arg_keys[6], 71), 0)
    out_grad = gaussian(arg_keys[1], (MICRO, SEQ, D), ((MICRO * SEQ) ** -0.5), 0.625, ((1, 4), (2, 4)))
    short_filters = gaussian(arg_keys[2], (LAYERS, 3, KS, D), KS ** -0.5, 2.0, ((0, 2), (3, 4)), jnp.float32)
    long_filters = gaussian(arg_keys[3], (LAYERS, KL, D), KL ** -0.5, 0.5, ((0, 2), (2, 4)), jnp.float32)
    skip_gain = jnp.clip(jax.random.uniform(arg_keys[4], (LAYERS, D), jnp.float32, -1.0, 1.0) * shard_levels(arg_keys[4], (LAYERS, D), ((0, 2), (1, 4)), -0.4, 0.0), -1.0, 1.0)
    norm_gain = jnp.clip(0.5 + 1.0 * jax.random.uniform(arg_keys[5], (LAYERS, D), jnp.float32) ** shard_levels(arg_keys[5], (LAYERS, D), ((0, 2), (1, 4)), -0.2, 0.2), 0.5, 1.5)
    return {"inputs": inputs, "out_grad": out_grad, "short_filters": short_filters, "long_filters": long_filters, "skip_gain": skip_gain, "norm_gain": norm_gain}


EPSILON = 1e-06

def causal(signal, filters):
    length = signal.shape[0]
    size = length + filters.shape[0]
    spectrum = jnp.fft.rfft(signal, size, axis=0) * jnp.fft.rfft(filters, size, axis=0)
    return jnp.fft.irfft(spectrum, size, axis=0)[:length]

def anticausal(signal, filters):
    return causal(signal[::-1], filters)[::-1]

def tap_sums(cotangent, signal, taps):
    length = signal.shape[0]
    size = 2 * length
    spectrum = jnp.fft.rfft(cotangent[::-1], size, axis=0) * jnp.fft.rfft(signal, size, axis=0)
    full = jnp.fft.irfft(spectrum, size, axis=0)[:length]
    return full[length - taps:][::-1]

def round_trip(values):
    return lax.optimization_barrier(values.astype(jnp.bfloat16)).astype(jnp.float32)

def layer_pieces(x_rows, shorts, longs, skip_row, gain_row):
    x_float = x_rows.astype(jnp.float32)
    scale = lax.rsqrt(lax.optimization_barrier(jnp.sum(x_float * x_float, axis=1)) / D + EPSILON)
    normed = round_trip(x_float * scale[:, None] * gain_row)
    query = causal(normed, shorts[0])
    key_rows = causal(normed, shorts[1])
    value_rows = causal(normed, shorts[2])
    mixed = round_trip(key_rows * value_rows)
    filtered = causal(mixed, longs) + skip_row * mixed
    return (x_float, scale, normed, query, key_rows, value_rows, mixed, filtered)

def reference(inputs, out_grad, short_filters, long_filters, skip_gain, norm_gain):
    layer_count = short_filters.shape[0]
    grad_list = [jnp.zeros((3 * KS + KL + 2, D), jnp.float32) for layer in range(layer_count)]
    for micro in range(MICRO):
        x_rows = inputs[micro]
        saved = []
        for layer in range(layer_count):
            saved.append(x_rows)
            pieces = layer_pieces(x_rows, short_filters[layer], long_filters[layer], skip_gain[layer], norm_gain[layer])
            x_rows = (pieces[0] + pieces[3] * pieces[7]).astype(jnp.bfloat16)
        cotangent = out_grad[micro]
        for layer in range(layer_count - 1, -1, -1):
            shorts = short_filters[layer]
            gain_row = norm_gain[layer]
            skip_row = skip_gain[layer]
            x_float, scale, normed, query, key_rows, value_rows, mixed, filtered = layer_pieces(saved[layer], shorts, long_filters[layer], skip_row, gain_row)
            e_float = cotangent.astype(jnp.float32)
            d_query = round_trip(e_float * filtered)
            d_filtered = round_trip(e_float * query)
            d_mixed = anticausal(d_filtered, long_filters[layer]) + skip_row * d_filtered
            d_key = round_trip(d_mixed * value_rows)
            d_value = round_trip(d_mixed * key_rows)
            d_normed = anticausal(d_query, shorts[0]) + anticausal(d_key, shorts[1]) + anticausal(d_value, shorts[2])
            fresh = jnp.concatenate([tap_sums(d_query, normed, KS), tap_sums(d_key, normed, KS), tap_sums(d_value, normed, KS), tap_sums(d_filtered, mixed, KL), lax.optimization_barrier(jnp.sum(d_filtered * mixed, axis=0))[None], lax.optimization_barrier(jnp.sum(d_normed * x_float * scale[:, None], axis=0))[None]], axis=0)
            grad_list[layer] = grad_list[layer] + fresh
            norm_term = lax.optimization_barrier(jnp.sum(gain_row * d_normed * x_float, axis=1)) / D
            cotangent = (e_float + scale[:, None] * gain_row * d_normed - x_float * (scale * scale * scale)[:, None] * norm_term[:, None]).astype(jnp.bfloat16)
    return jnp.stack(grad_list, axis=0)
```

```python
import functools

import jax
import jax.numpy as jnp
import numpy as np
from jax import lax
from jax.experimental import pallas as pl
from jax.experimental.pallas import tpu as pltpu
from jax.sharding import PartitionSpec as P

D = 4096


EPSILON = 1e-06


def shifted(block, axis, distance):
    devices = range(lax.axis_size(axis))
    route = [(i - distance, i) for i in devices if i - distance in devices]
    return lax.ppermute(block, axis, route)


def as_sent(array):
    return jax.tree.map(lambda a: a.astype(jnp.bfloat16) if a.dtype == jnp.float32 else a, array)


def correlate(signal, filters):
    result = lax.conv_general_dilated(
        signal[None],
        filters[:, None, :],
        (1,),
        "VALID",
        dimension_numbers=("NWC", "WIO", "NWC"),
        feature_group_count=signal.shape[1],
        precision=lax.Precision.HIGHEST,
    )
    return result[0]


def rows_before(source_rows, wanted, sender):
    row_count = source_rows.shape[0]
    hop_count = (wanted + row_count - 1) // row_count
    pieces = []
    for distance in range(hop_count, 0, -1):
        taking = min(row_count, wanted - (distance - 1) * row_count)
        pieces.append(sender(source_rows[row_count - taking :], distance))
    return jnp.concatenate(pieces, axis=0)


def rows_after(source_rows, wanted, sender):
    row_count = source_rows.shape[0]
    hop_count = (wanted + row_count - 1) // row_count
    pieces = []
    for distance in range(1, hop_count + 1):
        taking = min(row_count, wanted - (distance - 1) * row_count)
        pieces.append(sender(source_rows[:taking], distance))
    return jnp.concatenate(pieces, axis=0)


def forward_layer(x_rows, short_taps, long_taps, skip_row, gain_row):
    short_len = short_taps.shape[1]
    long_len = long_taps.shape[0]
    x_float = x_rows.astype(jnp.float32)
    squares = lax.psum(jnp.sum(x_float * x_float, axis=1), "chan")
    scale = lax.rsqrt(squares / D + EPSILON)
    normed = (x_float * scale[:, None] * gain_row).astype(jnp.bfloat16)
    h_before = rows_before(
        normed, short_len - 1, lambda shard_rows, distance: shifted(shard_rows, "seq", distance)
    )
    h_extended = jnp.concatenate([h_before, normed], axis=0)
    h_float = h_extended.astype(jnp.float32)
    query = correlate(h_float, short_taps[0][::-1])
    key_rows = correlate(h_float, short_taps[1][::-1])
    value_rows = correlate(h_float, short_taps[2][::-1])
    mixed = (key_rows * value_rows).astype(jnp.bfloat16)
    z_before = rows_before(
        mixed,
        long_len - 1,
        lambda shard_rows, distance: jax.tree.map(
            lambda part, own: part.astype(own.dtype),
            shifted(as_sent(shard_rows), "seq", distance),
            shard_rows,
        ),
    )
    z_extended = jnp.concatenate([z_before, mixed], axis=0)
    mixed_float = z_extended.astype(jnp.float32)
    filtered = correlate(mixed_float, long_taps[::-1]) + skip_row * mixed_float[long_len - 1 :]
    x_next = (x_float + query * filtered).astype(jnp.bfloat16)
    return (x_next, (x_rows, h_extended, z_extended, scale))


def backward_layer(e_rows, stored, short_taps, long_taps, skip_row, gain_row):
    short_len = short_taps.shape[1]
    long_len = long_taps.shape[0]
    x_bf, h_bf, z_bf, scale = stored
    row_count = x_bf.shape[0]
    x_float = x_bf.astype(jnp.float32)
    h_float = h_bf.astype(jnp.float32)
    z_float = z_bf.astype(jnp.float32)
    query = correlate(h_float, short_taps[0][::-1])
    key_rows = correlate(h_float, short_taps[1][::-1])
    value_rows = correlate(h_float, short_taps[2][::-1])
    mixed_float = z_float[long_len - 1 :]
    filtered = correlate(z_float, long_taps[::-1]) + skip_row * mixed_float
    e_float = e_rows.astype(jnp.float32)
    d_query = (e_float * filtered).astype(jnp.bfloat16)
    d_filtered = (e_float * query).astype(jnp.bfloat16)
    filtered_after = rows_after(
        d_filtered, long_len - 1, lambda shard_rows, distance: shifted(shard_rows, "seq", -distance)
    )
    filtered_float = jnp.concatenate([d_filtered, filtered_after], axis=0).astype(jnp.float32)
    d_mixed = correlate(filtered_float, long_taps) + skip_row * filtered_float[:row_count]
    d_key = (d_mixed * value_rows).astype(jnp.bfloat16)
    d_value = (d_mixed * key_rows).astype(jnp.bfloat16)
    streams = jnp.stack([d_query, d_key, d_value], axis=1)
    streams_after = rows_after(
        streams, short_len - 1, lambda shard_rows, distance: shifted(shard_rows, "seq", -distance)
    )
    streams_float = jnp.concatenate([streams, streams_after], axis=0).astype(jnp.float32)
    d_normed = correlate(streams_float[:, 0], short_taps[0])
    d_normed = d_normed + correlate(streams_float[:, 1], short_taps[1])
    d_normed = d_normed + correlate(streams_float[:, 2], short_taps[2])
    fresh = jnp.concatenate(
        [
            correlate(h_float, streams_float[:row_count, 0])[::-1],
            correlate(h_float, streams_float[:row_count, 1])[::-1],
            correlate(h_float, streams_float[:row_count, 2])[::-1],
            correlate(z_float, filtered_float[:row_count])[::-1],
            jnp.sum(filtered_float[:row_count] * mixed_float, axis=0)[None],
            jnp.sum(d_normed * x_float * scale[:, None], axis=0)[None],
        ],
        axis=0,
    )
    norm_term = lax.psum(jnp.sum(gain_row * d_normed * x_float, axis=1), "chan") / D
    e_prev = (
        e_float
        + scale[:, None] * gain_row * d_normed
        - x_float * (scale * scale * scale)[:, None] * norm_term[:, None]
    ).astype(jnp.bfloat16)
    return (e_prev, fresh)


def on_device(inputs, out_grad, short_filters, long_filters, skip_gain, norm_gain):
    sections = lax.axis_size("section")
    section_index = lax.axis_index("section")
    micro_count, row_count, channels = inputs.shape
    short_len = short_filters.shape[2]
    long_len = long_filters.shape[1]
    param_rows = 3 * short_len + long_len + 2
    gathered = (
        lax.all_gather(short_filters, "section", axis=0, tiled=True),
        lax.all_gather(long_filters, "section", axis=0, tiled=True),
        lax.all_gather(skip_gain, "section", axis=0, tiled=True),
        lax.all_gather(norm_gain, "section", axis=0, tiled=True),
    )
    layer_count = gathered[0].shape[0]
    per_device = micro_count // sections
    own_inputs = lax.dynamic_slice_in_dim(inputs, section_index * per_device, per_device, 0)
    own_grads = lax.dynamic_slice_in_dim(out_grad, section_index * per_device, per_device, 0)

    def one_micro(grad_total, micro_rows):
        first_rows, top_grad = micro_rows

        def forward_pass(x_rows, params):
            return forward_layer(x_rows, params[0], params[1], params[2], params[3])

        x_final, stored_all = lax.scan(forward_pass, first_rows, gathered)

        def backward_pass(e_rows, layer_items):
            params, stored = layer_items
            return backward_layer(e_rows, stored, params[0], params[1], params[2], params[3])

        e_first, fresh_all = lax.scan(backward_pass, top_grad, (gathered, stored_all), reverse=True)
        return (grad_total + fresh_all, None)

    grads_start = jnp.zeros((layer_count, param_rows, channels), jnp.float32)
    grads_done, unused_micro = lax.scan(one_micro, grads_start, (own_inputs, own_grads))
    local_grads = lax.psum_scatter(grads_done, "section", scatter_dimension=0, tiled=True)
    return lax.psum(local_grads, "seq")


F32, BF16 = jnp.float32, jnp.bfloat16
PAD = 8
CHUNK = 32


def split(value):
    high = value.astype(BF16)
    return high, (value - high.astype(F32)).astype(BF16)


def mm(a, b):
    return jnp.dot(a, b, preferred_element_type=F32)


def mm3(a_high, a_low, value):
    high, low = split(value)
    return mm(a_high, high) + (mm(a_high, low) + mm(a_low, high))


def lane_sums(value):
    high, low = split(value)
    both = jnp.concatenate([high, low], axis=1)
    ones = jnp.ones((16, both.shape[1]), BF16)
    sums = lax.dot_general(ones, both, (((1,), (1,)), ((), ())), preferred_element_type=F32)
    return sums[0:1]


def as_columns(row, width):
    return jnp.transpose(jnp.broadcast_to(row, (width, row.shape[1])))


def spectrum_size(rows, taps):
    return -(-(rows + taps) // 128) * 128


def spectrum_tables(rows, taps):
    size = spectrum_size(rows, taps)
    angle = (2 * np.pi / size) * (np.arange(size // 2)[:, None] + 0.5) * np.arange(rows)[None]
    forward = np.concatenate([np.cos(angle), -np.sin(angle)], axis=0)
    inverse = (2.0 / size) * forward.T

    def pair(table):
        table = table.astype(np.float32)
        high = table.astype(BF16)
        low = (table - high.astype(np.float32)).astype(BF16)
        return np.stack([high, low])

    return pair(forward), pair(inverse)


def channel_kernel(sizes, x_in, g_in, sf_in, lf_in, sk_in, ng_in, fw_in, iv_in, out,
                   x_own, x_all, g_all, sf, lf, sk, ng, fw, iv,
                   part0_out, part0, part_out, part, xf, scale, normed, query, key, value, mixed, m_hat,
                   filtered, f_hat, d_fil, d_hat, d_str, d_nor, e_one, fresh, fresh_out,
                   loc_sem, x_send, x_recv, f_send, f_recv, p0_send, p0_recv, p_send, p_recv, o_send, o_recv):
    S, Q, C, M, R, W, KS, KL, D = sizes
    T = Q * R
    N = spectrum_size(T, KL)
    H = N // 2
    L = S
    P_ALL = S * Q * C
    s, q, c = lax.axis_index("section"), lax.axis_index("seq"), lax.axis_index("chan")
    me = (s * Q + q) * C + c
    lane = lambda slot: pl.ds(pl.multiple_of(slot * W, W), W)
    rows_at = lambda seq: pl.ds(pl.multiple_of(seq * R, R), R)

    def at(section, seq, chan):
        return {"section": section, "seq": seq, "chan": chan}

    def peer(offset):
        p = lax.rem(me + offset, P_ALL)
        return p, at(p // (Q * C), (p // C) % Q, p % C)

    def remote(src, dst, send, recv, where):
        return pltpu.make_async_remote_copy(src_ref=src, dst_ref=dst, send_sem=send, recv_sem=recv,
                                            device_id=where, device_id_type=pl.DeviceIdType.MESH)

    own = q * S + s
    locals_ = [
        (x_in, x_own), (x_in.at[:, :, lane(own)], x_all.at[:, rows_at(q), :]),
        (g_in.at[:, :, lane(own)], g_all.at[:, rows_at(q), :]),
        (sf_in.at[:, :, :, lane(own)], sf.at[pl.ds(s, 1)]), (lf_in.at[:, :, lane(own)], lf.at[pl.ds(s, 1)]),
        (sk_in.at[:, lane(own)], sk.at[s]), (ng_in.at[:, lane(own)], ng.at[s]),
        (fw_in, fw), (iv_in, iv),
    ]
    local_copies = [pltpu.make_async_copy(a, b, loc_sem.at[i]) for i, (a, b) in enumerate(locals_)]
    for copy in local_copies:
        copy.start()

    barrier = pltpu.get_barrier_semaphore()

    def greet(offset, carry):
        pl.semaphore_signal(barrier, inc=1, device_id=peer(offset)[1], device_id_type=pl.DeviceIdType.MESH)
        return carry

    lax.fori_loop(1, P_ALL, greet, 0)

    local_copies[0].wait()
    for m in range(M):
        total = None
        for b in range(x_own.shape[2] // W):
            piece = x_own[m, :, b * W:(b + 1) * W].astype(F32)
            total = piece * piece if total is None else total + piece * piece
        d_nor[m, 0:R, :] = total
    gathered = jnp.concatenate([d_nor[m, 0:R, :] for m in range(M)], axis=0)
    part0_out[...] = lane_sums(gathered)

    pl.semaphore_wait(barrier, P_ALL - 1)

    def p0_slot(seq, chan):
        return seq * C + chan

    def p0_copy(offset):
        p = lax.rem(q * C + c + offset, Q * C)
        return remote(part0_out, part0.at[q * C + c], p0_send.at[p], p0_recv.at[q * C + c], at(s, p // C, p % C))

    def p0_start(offset, carry):
        p0_copy(offset).start()
        return carry

    lax.fori_loop(1, Q * C, p0_start, 0)
    x_copies, g_copies = [], []
    for offset in range(1, Q):
        to = lax.rem(q + offset, Q)
        src_slot = to * S + s
        x_copies.append(remote(x_in.at[:, :, lane(src_slot)], x_all.at[:, rows_at(q), :], x_send.at[0, offset], x_recv.at[0, offset], at(s, to, c)))
        g_copies.append(remote(g_in.at[:, :, lane(src_slot)], g_all.at[:, rows_at(q), :], x_send.at[1, offset], x_recv.at[1, offset], at(s, to, c)))
    for copy in x_copies:
        copy.start()
    mate = 1 - s
    theirs = q * S + mate
    f_copies = [
        remote(src, dst, f_send.at[i], f_recv.at[i], at(mate, q, c))
        for i, (src, dst) in enumerate([
            (sf_in.at[:, :, :, lane(theirs)], sf.at[pl.ds(s, 1)]), (lf_in.at[:, :, lane(theirs)], lf.at[pl.ds(s, 1)]),
            (sk_in.at[:, lane(theirs)], sk.at[s]), (ng_in.at[:, lane(theirs)], ng.at[s]),
        ])
    ]
    for copy in f_copies:
        copy.start()
    for copy in g_copies:
        copy.start()

    for l in range(L):
        for m in range(M):
            normed[l, m, 0:PAD, :] = jnp.zeros((PAD, W), F32)
    for i in range(3):
        for m in range(M):
            d_str[i, m, T:T + PAD, :] = jnp.zeros((PAD, W), F32)
    for copy in local_copies[1:]:
        copy.wait()
    for copy in f_copies:
        copy.wait()
    for l in range(L):
        f_hat[l] = mm3(fw[0, :, 0:KL], fw[1, :, 0:KL], lf[l])
        f_hat[l, 0:H, :] = f_hat[l, 0:H, :] + sk[l]

    def p0_wait(offset, carry):
        p = lax.rem(q * C + c + offset, Q * C)
        remote(part0_out, part0.at[p], p0_send.at[p], p0_recv.at[p], at(s, p // C, p % C)).wait_recv()
        return carry

    part0[q * C + c] = part0_out[...]
    lax.fori_loop(1, Q * C, p0_wait, 0)
    for seq in range(Q):
        row = part0[seq * C]
        for chan in range(1, C):
            row = row + part0[seq * C + chan]
        columns = as_columns(lax.rsqrt(row / D + EPSILON), W)
        for m in range(M):
            scale[0, m, seq * R:(seq + 1) * R, :] = columns[m * R:(m + 1) * R]
    for copy in x_copies:
        copy.wait_recv()
    for m in range(M):
        for t in range(0, T, R):
            xf[0, m, t:t + R, :] = x_all[m, t:t + R, :].astype(F32)

    def chunks(body):
        def step(i, carry):
            body(pl.multiple_of(i * CHUNK, CHUNK))
            return carry

        lax.fori_loop(0, T // CHUNK, step, 0)

    def rounded(v):
        return v.astype(BF16).astype(F32)

    def forward(l):
        gain = ng[l]
        for m in range(M):
            def norm_chunk(t):
                v = xf[l, m, pl.ds(t, CHUNK), :] * scale[l, m, pl.ds(t, CHUNK), :] * gain
                normed[l, m, pl.ds(t + PAD, CHUNK), :] = rounded(v)

            chunks(norm_chunk)
        taps = [[sf[l, i, j:j + 1, :] for j in range(KS)] for i in range(3)]
        for m in range(M):
            def short_chunk(t):
                sums = [None] * 3
                for j in range(KS):
                    shifted_rows = normed[l, m, pl.ds(t + PAD - j, CHUNK), :]
                    for i in range(3):
                        term = taps[i][j] * shifted_rows
                        sums[i] = term if sums[i] is None else sums[i] + term
                query[l, m, pl.ds(t, CHUNK), :] = sums[0]
                key[l, m, pl.ds(t, CHUNK), :] = sums[1]
                value[l, m, pl.ds(t, CHUNK), :] = sums[2]
                mixed[pl.ds(t, CHUNK), m * W:(m + 1) * W] = (sums[1] * sums[2]).astype(BF16)

            chunks(short_chunk)
        m_hat[l] = mm(fw[0], mixed[...]) + mm(fw[1], mixed[...])
        pieces = []
        for m in range(M):
            fr, fi = f_hat[l, 0:H, :], f_hat[l, H:N, :]
            mr, mi = m_hat[l, 0:H, m * W:(m + 1) * W], m_hat[l, H:N, m * W:(m + 1) * W]
            pieces.append(jnp.concatenate([fr * mr - fi * mi, fr * mi + fi * mr], axis=0))
        result = mm3(iv[0], iv[1], jnp.concatenate(pieces, axis=1))
        for m in range(M):
            filtered[l, m] = result[:, m * W:(m + 1) * W]

    def exchange(stage, rows_of):
        part_out[stage] = jnp.concatenate([lane_sums(rows_of(m)) for m in range(M)], axis=1)

        def send(offset, carry):
            p, where = peer(offset)
            remote(part_out.at[stage], part.at[stage, me], p_send.at[stage, p], p_recv.at[stage, me], where).start()
            return carry

        lax.fori_loop(1, P_ALL, send, 0)

    def exchanged(stage):
        part[stage, me] = part_out[stage]

        def wait(offset, carry):
            p, where = peer(offset)
            remote(part_out.at[stage], part.at[stage, p], p_send.at[stage, p], p_recv.at[stage, p], where).wait_recv()
            return carry

        lax.fori_loop(1, P_ALL, wait, 0)
        rows = [part[stage, p] for p in range(P_ALL)]
        while len(rows) > 1:
            rows = [a + b for a, b in zip(rows[::2], rows[1::2])] + ([rows[-1]] if len(rows) % 2 else [])
        return rows[0]

    for l in range(L):
        forward(l)
        if l < L - 1:
            for m in range(M):
                xf[l + 1, m] = rounded(xf[l, m] + query[l, m] * filtered[l, m])
            exchange(l, lambda m: xf[l + 1, m] * xf[l + 1, m])
            root = lax.rsqrt(exchanged(l) / D + EPSILON)
            for m in range(M):
                scale[l + 1, m] = as_columns(root[:, m * T:(m + 1) * T], W)

    for copy in g_copies:
        copy.wait_recv()

    def send_rows(l, part_index, low, high):
        for seq in range(Q):
            here = jnp.logical_and(s == l, q == seq)

            @pl.when(here)
            def _():
                out[low:high, lane(own)] = fresh_out[l, low:high, :]

            @pl.when(jnp.logical_not(here))
            def _():
                remote(fresh_out.at[l, low:high, :], out.at[low:high, lane(own)], o_send.at[l, part_index, seq],
                       o_recv.at[part_index, own], at(l, seq, c)).start()

    rows_total = 3 * KS + KL + 2
    early_low = -(-3 * KS // 16) * 16
    early_high = (3 * KS + KL) // 16 * 16
    late_high = fresh_out.shape[1]
    spans = [(early_low, early_high), (0, early_low), (early_high, late_high)]
    stages = L - 1
    for l in reversed(range(L)):
        top = l == L - 1
        for m in range(M):
            e = g_all[m].astype(F32) if top else e_one[m]
            d_str[0, m, 0:T, :] = rounded(e * filtered[l, m])
            d_fil[:, m * W:(m + 1) * W] = (e * query[l, m]).astype(BF16)
        d_hat[...] = mm(fw[0], d_fil[...]) + mm(fw[1], d_fil[...])

        def long_gradient():
            re, im = None, None
            for m in range(M):
                dr, di = d_hat[0:H, m * W:(m + 1) * W], d_hat[H:N, m * W:(m + 1) * W]
                mr, mi = m_hat[l, 0:H, m * W:(m + 1) * W], m_hat[l, H:N, m * W:(m + 1) * W]
                a, b = dr * mr + di * mi, di * mr - dr * mi
                re, im = (a, b) if re is None else (re + a, im + b)
            taps_grad = mm3(iv[0, 0:KL, :], iv[1, 0:KL, :], jnp.concatenate([re, im], axis=0))
            fresh[3 * KS:3 * KS + KL, :] = taps_grad
            fresh[3 * KS + KL:3 * KS + KL + 1, :] = taps_grad[0:1]
            fresh_out[l, early_low:early_high, :] = fresh[early_low:early_high, :].astype(BF16)
            send_rows(l, 0, early_low, early_high)

        if not top:
            long_gradient()
        pieces = []
        for m in range(M):
            fr, fi = f_hat[l, 0:H, :], f_hat[l, H:N, :]
            dr, di = d_hat[0:H, m * W:(m + 1) * W], d_hat[H:N, m * W:(m + 1) * W]
            pieces.append(jnp.concatenate([fr * dr + fi * di, fr * di - fi * dr], axis=0))
        d_mix = mm3(iv[0], iv[1], jnp.concatenate(pieces, axis=1))
        for m in range(M):
            d_mix_m = d_mix[:, m * W:(m + 1) * W]
            d_str[1, m, 0:T, :] = rounded(d_mix_m * value[l, m])
            d_str[2, m, 0:T, :] = rounded(d_mix_m * key[l, m])
        taps = [[sf[l, i, j:j + 1, :] for j in range(KS)] for i in range(3)]
        for m in range(M):
            def normed_chunk(t):
                total = None
                for i in range(3):
                    for j in range(KS):
                        term = taps[i][j] * d_str[i, m, pl.ds(t + j, CHUNK), :]
                        total = term if total is None else total + term
                d_nor[m, pl.ds(t, CHUNK), :] = total

            chunks(normed_chunk)
        gain = ng[l]
        if l > 0:
            exchange(stages, lambda m: gain * d_nor[m] * xf[l, m])
        if top:
            long_gradient()
        fold = lambda v: jnp.sum(v.reshape(CHUNK // 8, 8, W), axis=0)
        zeros = tuple(jnp.zeros((8, W), F32) for _ in range(3 * KS + 1))

        def grad_chunk(i, carry):
            t = pl.multiple_of(i * CHUNK, CHUNK)
            sums = list(carry)
            for m in range(M):
                streams = [d_str[k, m, pl.ds(t, CHUNK), :] for k in range(3)]
                for j in range(KS):
                    shifted_rows = normed[l, m, pl.ds(t + PAD - j, CHUNK), :]
                    for k in range(3):
                        sums[k * KS + j] = sums[k * KS + j] + fold(streams[k] * shifted_rows)
                gain_terms = d_nor[m, pl.ds(t, CHUNK), :] * xf[l, m, pl.ds(t, CHUNK), :] * scale[l, m, pl.ds(t, CHUNK), :]
                sums[3 * KS] = sums[3 * KS] + fold(gain_terms)
            return tuple(sums)

        sums = lax.fori_loop(0, T // CHUNK, grad_chunk, zeros)
        for row in range(3 * KS):
            fresh[row:row + 1, :] = jnp.sum(sums[row], axis=0, keepdims=True)
        fresh[rows_total - 1:rows_total, :] = jnp.sum(sums[3 * KS], axis=0, keepdims=True)
        for index in (1, 2):
            low, high = spans[index]
            fresh_out[l, low:high, :] = fresh[low:high, :].astype(BF16)
            send_rows(l, index, low, high)
        if l > 0:
            norm_row = exchanged(stages) / D
            for m in range(M):
                term = as_columns(norm_row[:, m * T:(m + 1) * T], W)
                r = scale[l, m]
                e_one[m] = rounded(g_all[m].astype(F32) + r * gain * d_nor[m] - xf[l, m] * (r * r * r) * term)

    for seq in range(Q):
        for sec in range(S):
            slot = seq * S + sec
            here = jnp.logical_and(s == sec, q == seq)

            @pl.when(jnp.logical_not(here))
            def _():
                for index, (low, high) in enumerate(spans):
                    remote(fresh_out.at[0, low:high, :], out.at[low:high, slot * W:(slot + 1) * W], o_send.at[0, index, 0],
                           o_recv.at[index, slot], at(s, q, c)).wait_recv()
    for l in range(L):
        for seq in range(Q):
            here = jnp.logical_and(s == l, q == seq)

            @pl.when(jnp.logical_not(here))
            def _():
                for index, (low, high) in enumerate(spans):
                    remote(fresh_out.at[l, low:high, :], out.at[low:high, lane(own)], o_send.at[l, index, seq],
                           o_recv.at[index, own], at(l, seq, c)).wait_send()
    for copy in x_copies + g_copies:
        copy.wait_send()

    def p0_sent(offset, carry):
        p0_copy(offset).wait_send()
        return carry

    lax.fori_loop(1, Q * C, p0_sent, 0)
    for stage in range(L):
        def sent(offset, carry):
            p, where = peer(offset)
            remote(part_out.at[stage], part.at[stage, me], p_send.at[stage, p], p_recv.at[stage, me], where).wait_send()
            return carry

        lax.fori_loop(1, P_ALL, sent, 0)


def kernel_fits(mesh, args):
    x, sf, lf = args[0], args[2], args[3]
    S, Q = mesh.shape["section"], mesh.shape["seq"]
    width = x.shape[2] // (S * Q)
    rows = Q * x.shape[1]
    return (S == 2 and sf.shape[0] == 1 and width * S * Q == x.shape[2] and width == 128
            and x.shape[1] % CHUNK == 0 and x.shape[0] * x.shape[1] == 128 and sf.shape[2] <= PAD
            and lf.shape[1] % 128 == 0 and lf.shape[1] <= rows)


def by_channels(mesh, x, g, sf, lf, sk, ng):
    S, Q, C = mesh.shape["section"], mesh.shape["seq"], mesh.shape["chan"]
    M, R, channels = x.shape
    KS, KL = sf.shape[2], lf.shape[1]
    W, T, L, G = channels // (S * Q), Q * R, S, S * Q * C
    N = spectrum_size(T, KL)
    fw, iv = spectrum_tables(T, KL)
    rows_total = 3 * KS + KL + 2
    rows_out = -(-rows_total // 16) * 16
    V, dma = pltpu.VMEM, pltpu.SemaphoreType.DMA
    sizes = (S, Q, C, M, R, W, KS, KL, D)
    big = lambda: V((L, M, T, W), F32)
    spans = 3
    result = pl.pallas_call(
        functools.partial(channel_kernel, sizes),
        out_shape=jax.ShapeDtypeStruct((rows_out, channels), BF16),
        in_specs=[pl.BlockSpec(memory_space=pl.ANY)] * 8,
        out_specs=pl.BlockSpec(memory_space=pltpu.VMEM),
        scratch_shapes=[
            V((M, R, channels), BF16), V((M, T, W), BF16), V((M, T, W), BF16),
            V((L, 3, KS, W), F32), V((L, KL, W), F32), V((L, 1, W), F32), V((L, 1, W), F32),
            V(fw.shape, BF16), V(iv.shape, BF16),
            V((1, M * R), F32), V((Q * C, 1, M * R), F32), V((L, 1, M * T), F32), V((L, G, 1, M * T), F32),
            big(), big(), V((L, M, PAD + T, W), F32), big(), big(), big(),
            V((T, M * W), BF16), V((L, N, M * W), F32), big(), V((L, N, W), F32),
            V((T, M * W), BF16), V((N, M * W), F32), V((3, M, T + PAD, W), F32), V((M, T, W), F32),
            V((M, T, W), F32), V((rows_out, W), F32), V((L, rows_out, W), BF16),
            dma((9,)), dma((2, Q)), dma((2, Q)), dma((4,)), dma((4,)), dma((Q * C,)), dma((Q * C,)),
            dma((L, G)), dma((L, G)), dma((L, spans, Q)), dma((spans, S * Q)),
        ],
        compiler_params=pltpu.CompilerParams(collective_id=0, has_side_effects=True, vmem_limit_bytes=40 * 1024 * 1024),
    )(x, g, sf, lf, sk, ng, jnp.asarray(fw), jnp.asarray(iv))
    return result[:rows_total].astype(F32)[None]


def solution(mesh):
    placed = (
        P(None, "seq", "chan"),
        P(None, "seq", "chan"),
        P("section", None, None, "chan"),
        P("section", None, "chan"),
        P("section", "chan"),
        P("section", "chan"),
    )

    def body(*args):
        if kernel_fits(mesh, args):
            return by_channels(mesh, *args)
        return on_device(*args)

    return jax.shard_map(
        body, mesh=mesh, in_specs=placed, out_specs=P("section", None, "chan"), check_vma=False
    )
```

```python
import functools

import jax
import jax.numpy as jnp
import numpy as np
from jax import lax
from jax.experimental import pallas as pl
from jax.experimental.pallas import tpu as pltpu
from jax.sharding import PartitionSpec as P

D = 4096


EPSILON = 1e-06


def shifted(block, axis, distance):
    devices = range(lax.axis_size(axis))
    route = [(i - distance, i) for i in devices if i - distance in devices]
    return lax.ppermute(block, axis, route)


def as_sent(array):
    return jax.tree.map(lambda a: a.astype(jnp.bfloat16) if a.dtype == jnp.float32 else a, array)


def correlate(signal, filters):
    result = lax.conv_general_dilated(
        signal[None],
        filters[:, None, :],
        (1,),
        "VALID",
        dimension_numbers=("NWC", "WIO", "NWC"),
        feature_group_count=signal.shape[1],
        precision=lax.Precision.HIGHEST,
    )
    return result[0]


def rows_before(source_rows, wanted, sender):
    row_count = source_rows.shape[0]
    hop_count = (wanted + row_count - 1) // row_count
    pieces = []
    for distance in range(hop_count, 0, -1):
        taking = min(row_count, wanted - (distance - 1) * row_count)
        pieces.append(sender(source_rows[row_count - taking :], distance))
    return jnp.concatenate(pieces, axis=0)


def rows_after(source_rows, wanted, sender):
    row_count = source_rows.shape[0]
    hop_count = (wanted + row_count - 1) // row_count
    pieces = []
    for distance in range(1, hop_count + 1):
        taking = min(row_count, wanted - (distance - 1) * row_count)
        pieces.append(sender(source_rows[:taking], distance))
    return jnp.concatenate(pieces, axis=0)


def forward_layer(x_rows, short_taps, long_taps, skip_row, gain_row):
    short_len = short_taps.shape[1]
    long_len = long_taps.shape[0]
    x_float = x_rows.astype(jnp.float32)
    squares = lax.psum(jnp.sum(x_float * x_float, axis=1), "chan")
    scale = lax.rsqrt(squares / D + EPSILON)
    normed = (x_float * scale[:, None] * gain_row).astype(jnp.bfloat16)
    h_before = rows_before(
        normed, short_len - 1, lambda shard_rows, distance: shifted(shard_rows, "seq", distance)
    )
    h_extended = jnp.concatenate([h_before, normed], axis=0)
    h_float = h_extended.astype(jnp.float32)
    query = correlate(h_float, short_taps[0][::-1])
    key_rows = correlate(h_float, short_taps[1][::-1])
    value_rows = correlate(h_float, short_taps[2][::-1])
    mixed = (key_rows * value_rows).astype(jnp.bfloat16)
    z_before = rows_before(
        mixed,
        long_len - 1,
        lambda shard_rows, distance: jax.tree.map(
            lambda part, own: part.astype(own.dtype),
            shifted(as_sent(shard_rows), "seq", distance),
            shard_rows,
        ),
    )
    z_extended = jnp.concatenate([z_before, mixed], axis=0)
    mixed_float = z_extended.astype(jnp.float32)
    filtered = correlate(mixed_float, long_taps[::-1]) + skip_row * mixed_float[long_len - 1 :]
    x_next = (x_float + query * filtered).astype(jnp.bfloat16)
    return (x_next, (x_rows, h_extended, z_extended, scale))


def backward_layer(e_rows, stored, short_taps, long_taps, skip_row, gain_row):
    short_len = short_taps.shape[1]
    long_len = long_taps.shape[0]
    x_bf, h_bf, z_bf, scale = stored
    row_count = x_bf.shape[0]
    x_float = x_bf.astype(jnp.float32)
    h_float = h_bf.astype(jnp.float32)
    z_float = z_bf.astype(jnp.float32)
    query = correlate(h_float, short_taps[0][::-1])
    key_rows = correlate(h_float, short_taps[1][::-1])
    value_rows = correlate(h_float, short_taps[2][::-1])
    mixed_float = z_float[long_len - 1 :]
    filtered = correlate(z_float, long_taps[::-1]) + skip_row * mixed_float
    e_float = e_rows.astype(jnp.float32)
    d_query = (e_float * filtered).astype(jnp.bfloat16)
    d_filtered = (e_float * query).astype(jnp.bfloat16)
    filtered_after = rows_after(
        d_filtered, long_len - 1, lambda shard_rows, distance: shifted(shard_rows, "seq", -distance)
    )
    filtered_float = jnp.concatenate([d_filtered, filtered_after], axis=0).astype(jnp.float32)
    d_mixed = correlate(filtered_float, long_taps) + skip_row * filtered_float[:row_count]
    d_key = (d_mixed * value_rows).astype(jnp.bfloat16)
    d_value = (d_mixed * key_rows).astype(jnp.bfloat16)
    streams = jnp.stack([d_query, d_key, d_value], axis=1)
    streams_after = rows_after(
        streams, short_len - 1, lambda shard_rows, distance: shifted(shard_rows, "seq", -distance)
    )
    streams_float = jnp.concatenate([streams, streams_after], axis=0).astype(jnp.float32)
    d_normed = correlate(streams_float[:, 0], short_taps[0])
    d_normed = d_normed + correlate(streams_float[:, 1], short_taps[1])
    d_normed = d_normed + correlate(streams_float[:, 2], short_taps[2])
    fresh = jnp.concatenate(
        [
            correlate(h_float, streams_float[:row_count, 0])[::-1],
            correlate(h_float, streams_float[:row_count, 1])[::-1],
            correlate(h_float, streams_float[:row_count, 2])[::-1],
            correlate(z_float, filtered_float[:row_count])[::-1],
            jnp.sum(filtered_float[:row_count] * mixed_float, axis=0)[None],
            jnp.sum(d_normed * x_float * scale[:, None], axis=0)[None],
        ],
        axis=0,
    )
    norm_term = lax.psum(jnp.sum(gain_row * d_normed * x_float, axis=1), "chan") / D
    e_prev = (
        e_float
        + scale[:, None] * gain_row * d_normed
        - x_float * (scale * scale * scale)[:, None] * norm_term[:, None]
    ).astype(jnp.bfloat16)
    return (e_prev, fresh)


def on_device(inputs, out_grad, short_filters, long_filters, skip_gain, norm_gain):
    sections = lax.axis_size("section")
    section_index = lax.axis_index("section")
    micro_count, row_count, channels = inputs.shape
    short_len = short_filters.shape[2]
    long_len = long_filters.shape[1]
    param_rows = 3 * short_len + long_len + 2
    gathered = (
        lax.all_gather(short_filters, "section", axis=0, tiled=True),
        lax.all_gather(long_filters, "section", axis=0, tiled=True),
        lax.all_gather(skip_gain, "section", axis=0, tiled=True),
        lax.all_gather(norm_gain, "section", axis=0, tiled=True),
    )
    layer_count = gathered[0].shape[0]
    per_device = micro_count // sections
    own_inputs = lax.dynamic_slice_in_dim(inputs, section_index * per_device, per_device, 0)
    own_grads = lax.dynamic_slice_in_dim(out_grad, section_index * per_device, per_device, 0)

    def one_micro(grad_total, micro_rows):
        first_rows, top_grad = micro_rows

        def forward_pass(x_rows, params):
            return forward_layer(x_rows, params[0], params[1], params[2], params[3])

        x_final, stored_all = lax.scan(forward_pass, first_rows, gathered)

        def backward_pass(e_rows, layer_items):
            params, stored = layer_items
            return backward_layer(e_rows, stored, params[0], params[1], params[2], params[3])

        e_first, fresh_all = lax.scan(backward_pass, top_grad, (gathered, stored_all), reverse=True)
        return (grad_total + fresh_all, None)

    grads_start = jnp.zeros((layer_count, param_rows, channels), jnp.float32)
    grads_done, unused_micro = lax.scan(one_micro, grads_start, (own_inputs, own_grads))
    local_grads = lax.psum_scatter(grads_done, "section", scatter_dimension=0, tiled=True)
    return lax.psum(local_grads, "seq")


F32, BF16 = jnp.float32, jnp.bfloat16
PAD = 8
CHUNK = 32


def split(value):
    high = value.astype(BF16)
    return high, (value - high.astype(F32)).astype(BF16)


def mm(a, b):
    return jnp.dot(a, b, preferred_element_type=F32)


def mm3(a_high, a_low, value):
    high, low = split(value)
    return mm(a_high, high) + (mm(a_high, low) + mm(a_low, high))


def lane_sums(value):
    high, low = split(value)
    both = jnp.concatenate([high, low], axis=1)
    ones = jnp.ones((16, both.shape[1]), BF16)
    sums = lax.dot_general(ones, both, (((1,), (1,)), ((), ())), preferred_element_type=F32)
    return sums[0:1]


def as_columns(row, width):
    return jnp.transpose(jnp.broadcast_to(row, (width, row.shape[1])))


def spectrum_size(rows, taps):
    return -(-(rows + taps) // 128) * 128


def spectrum_tables(rows, taps):
    size = spectrum_size(rows, taps)
    angle = (2 * np.pi / size) * (np.arange(size // 2)[:, None] + 0.5) * np.arange(rows)[None]
    forward = np.concatenate([np.cos(angle), -np.sin(angle)], axis=0)
    inverse = (2.0 / size) * forward.T

    def pair(table):
        table = table.astype(np.float32)
        high = table.astype(BF16)
        low = (table - high.astype(np.float32)).astype(BF16)
        return np.stack([high, low])

    return pair(forward), pair(inverse)


def channel_kernel(sizes, x_in, g_in, sf_in, lf_in, sk_in, ng_in, fw_in, iv_in, out,
                   x_own, x_all, g_all, sf, lf, sk, ng, fw, iv,
                   part0_out, part0, part_out, part, xf, scale, normed, query, key, value, mixed, m_hat,
                   filtered, f_hat, d_fil, d_hat, d_str, d_nor, e_one, fresh, fresh_out, arrived,
                   loc_sem, x_send, x_recv, f_send, f_recv, p0_send, p0_recv, p_send, p_recv, o_send, o_recv):
    S, Q, C, M, R, W, KS, KL, D = sizes
    T = Q * R
    N = spectrum_size(T, KL)
    H = N // 2
    L = S
    P_ALL = S * Q * C
    s, q, c = lax.axis_index("section"), lax.axis_index("seq"), lax.axis_index("chan")
    me = (s * Q + q) * C + c
    lane = lambda slot: pl.ds(pl.multiple_of(slot * W, W), W)
    rows_at = lambda seq: pl.ds(pl.multiple_of(seq * R, R), R)

    def at(section, seq, chan):
        return {"section": section, "seq": seq, "chan": chan}

    def peer(offset):
        p = lax.rem(me + offset, P_ALL)
        return p, at(p // (Q * C), (p // C) % Q, p % C)

    def remote(src, dst, send, recv, where):
        return pltpu.make_async_remote_copy(src_ref=src, dst_ref=dst, send_sem=send, recv_sem=recv,
                                            device_id=where, device_id_type=pl.DeviceIdType.MESH)

    own = q * S + s
    locals_ = [
        (x_in, x_own), (x_in.at[:, :, lane(own)], x_all.at[:, rows_at(q), :]),
        (g_in.at[:, :, lane(own)], g_all.at[:, rows_at(q), :]),
        (sf_in.at[:, :, lane(own)], sf.at[s]), (lf_in.at[:, :, lane(own)], lf.at[pl.ds(s, 1)]),
        (sk_in.at[:, lane(own)], sk.at[s]), (ng_in.at[:, lane(own)], ng.at[s]),
        (fw_in, fw), (iv_in, iv),
    ]
    local_copies = [pltpu.make_async_copy(a, b, loc_sem.at[i]) for i, (a, b) in enumerate(locals_)]
    for copy in local_copies:
        copy.start()

    barrier = pltpu.get_barrier_semaphore()

    def greet(offset, carry):
        pl.semaphore_signal(barrier, inc=1, device_id=peer(offset)[1], device_id_type=pl.DeviceIdType.MESH)
        return carry

    lax.fori_loop(1, P_ALL, greet, 0)

    local_copies[0].wait()
    for m in range(M):
        total = None
        for b in range(x_own.shape[2] // W):
            piece = x_own[m, :, b * W:(b + 1) * W].astype(F32)
            total = piece * piece if total is None else total + piece * piece
        d_nor[m, 0:R, :] = total
    gathered = jnp.concatenate([d_nor[m, 0:R, :] for m in range(M)], axis=0)
    part0_out[...] = lane_sums(gathered)

    pl.semaphore_wait(barrier, P_ALL - 1)

    def p0_slot(seq, chan):
        return seq * C + chan

    def p0_copy(offset):
        p = lax.rem(q * C + c + offset, Q * C)
        return remote(part0_out, part0.at[q * C + c], p0_send.at[p], p0_recv.at[q * C + c], at(s, p // C, p % C))

    def p0_start(offset, carry):
        p0_copy(offset).start()
        return carry

    lax.fori_loop(1, Q * C, p0_start, 0)
    x_copies, g_copies = [], []
    for offset in range(1, Q):
        to = lax.rem(q + offset, Q)
        src_slot = to * S + s
        x_copies.append(remote(x_in.at[:, :, lane(src_slot)], x_all.at[:, rows_at(q), :], x_send.at[0, offset], x_recv.at[0, offset], at(s, to, c)))
        g_copies.append(remote(g_in.at[:, :, lane(src_slot)], g_all.at[:, rows_at(q), :], x_send.at[1, offset], x_recv.at[1, offset], at(s, to, c)))
    for copy in x_copies:
        copy.start()
    mate = 1 - s
    theirs = q * S + mate
    f_copies = [
        remote(src, dst, f_send.at[i], f_recv.at[i], at(mate, q, c))
        for i, (src, dst) in enumerate([
            (sf_in.at[:, :, lane(theirs)], sf.at[s]), (lf_in.at[:, :, lane(theirs)], lf.at[pl.ds(s, 1)]),
            (sk_in.at[:, lane(theirs)], sk.at[s]), (ng_in.at[:, lane(theirs)], ng.at[s]),
        ])
    ]
    for copy in f_copies:
        copy.start()
    for copy in g_copies:
        copy.start()

    for l in range(L):
        for m in range(M):
            normed[l, m, 0:PAD, :] = jnp.zeros((PAD, W), F32)
    for i in range(3):
        for m in range(M):
            d_str[i, m, T:T + PAD, :] = jnp.zeros((PAD, W), F32)
    for copy in local_copies[1:]:
        copy.wait()
    for copy in f_copies:
        copy.wait()
    for l in range(L):
        f_hat[l] = mm3(fw[0, :, 0:KL], fw[1, :, 0:KL], lf[l])
        f_hat[l, 0:H, :] = f_hat[l, 0:H, :] + sk[l]

    def p0_wait(offset, carry):
        p = lax.rem(q * C + c + offset, Q * C)
        remote(part0_out, part0.at[p], p0_send.at[p], p0_recv.at[p], at(s, p // C, p % C)).wait_recv()
        return carry

    part0[q * C + c] = part0_out[...]
    lax.fori_loop(1, Q * C, p0_wait, 0)
    for seq in range(Q):
        row = part0[seq * C]
        for chan in range(1, C):
            row = row + part0[seq * C + chan]
        columns = as_columns(lax.rsqrt(row / D + EPSILON), W)
        for m in range(M):
            scale[0, m, seq * R:(seq + 1) * R, :] = columns[m * R:(m + 1) * R]
    for copy in x_copies:
        copy.wait_recv()
    for m in range(M):
        for t in range(0, T, R):
            xf[0, m, t:t + R, :] = x_all[m, t:t + R, :].astype(F32)

    def chunks(body):
        def step(i, carry):
            body(pl.multiple_of(i * CHUNK, CHUNK))
            return carry

        lax.fori_loop(0, T // CHUNK, step, 0)

    def rounded(v):
        return v.astype(BF16).astype(F32)

    def forward(l):
        gain = ng[l]
        for m in range(M):
            def norm_chunk(t):
                v = xf[l, m, pl.ds(t, CHUNK), :] * scale[l, m, pl.ds(t, CHUNK), :] * gain
                normed[l, m, pl.ds(t + PAD, CHUNK), :] = rounded(v)

            chunks(norm_chunk)
        taps = [[sf[l, i * KS + j] for j in range(KS)] for i in range(3)]
        for m in range(M):
            def short_chunk(t):
                sums = [None] * 3
                for j in range(KS):
                    shifted_rows = normed[l, m, pl.ds(t + PAD - j, CHUNK), :]
                    for i in range(3):
                        term = taps[i][j] * shifted_rows
                        sums[i] = term if sums[i] is None else sums[i] + term
                query[l, m, pl.ds(t, CHUNK), :] = sums[0]
                key[l, m, pl.ds(t, CHUNK), :] = sums[1]
                value[l, m, pl.ds(t, CHUNK), :] = sums[2]
                mixed[pl.ds(t, CHUNK), m * W:(m + 1) * W] = (sums[1] * sums[2]).astype(BF16)

            chunks(short_chunk)
        m_hat[l] = mm(fw[0], mixed[...]) + mm(fw[1], mixed[...])
        pieces = []
        for m in range(M):
            fr, fi = f_hat[l, 0:H, :], f_hat[l, H:N, :]
            mr, mi = m_hat[l, 0:H, m * W:(m + 1) * W], m_hat[l, H:N, m * W:(m + 1) * W]
            pieces.append(jnp.concatenate([fr * mr - fi * mi, fr * mi + fi * mr], axis=0))
        result = mm3(iv[0], iv[1], jnp.concatenate(pieces, axis=1))
        for m in range(M):
            filtered[l, m] = result[:, m * W:(m + 1) * W]

    def exchange(stage, rows_of):
        part_out[stage] = jnp.concatenate([lane_sums(rows_of(m)) for m in range(M)], axis=1)

        def send(offset, carry):
            p, where = peer(offset)
            remote(part_out.at[stage], part.at[stage, me], p_send.at[stage, p], p_recv.at[stage, me], where).start()
            return carry

        lax.fori_loop(1, P_ALL, send, 0)

    def exchanged(stage):
        part[stage, me] = part_out[stage]

        def wait(offset, carry):
            p, where = peer(offset)
            remote(part_out.at[stage], part.at[stage, p], p_send.at[stage, p], p_recv.at[stage, p], where).wait_recv()
            return carry

        lax.fori_loop(1, P_ALL, wait, 0)
        rows = [part[stage, p] for p in range(P_ALL)]
        while len(rows) > 1:
            rows = [a + b for a, b in zip(rows[::2], rows[1::2])] + ([rows[-1]] if len(rows) % 2 else [])
        return rows[0]

    for l in range(L):
        forward(l)
        if l < L - 1:
            for m in range(M):
                xf[l + 1, m] = rounded(xf[l, m] + query[l, m] * filtered[l, m])
            exchange(l, lambda m: xf[l + 1, m] * xf[l + 1, m])
            root = lax.rsqrt(exchanged(l) / D + EPSILON)
            for m in range(M):
                scale[l + 1, m] = as_columns(root[:, m * T:(m + 1) * T], W)

    for copy in g_copies:
        copy.wait_recv()

    slots = S * Q
    rows_total = 3 * KS + KL + 2

    def place(slot, low, high, values):
        high = min(high, rows_total)
        out[pl.ds(low * slots + slot, high - low, stride=slots), :] = values[0:high - low]

    def send_rows(l, part_index, low, high):
        for seq in range(Q):
            here = jnp.logical_and(s == l, q == seq)

            @pl.when(here)
            def _():
                place(own, low, high, fresh[low:high, :])

            @pl.when(jnp.logical_not(here))
            def _():
                remote(fresh_out.at[l, low:high, :], arrived.at[own, low:high, :], o_send.at[l, part_index, seq],
                       o_recv.at[part_index, own], at(l, seq, c)).start()

    early_low = -(-3 * KS // 16) * 16
    early_high = (3 * KS + KL) // 16 * 16
    late_high = fresh_out.shape[1]
    spans = [(early_low, early_high), (0, early_low), (early_high, late_high)]
    stages = L - 1
    for l in reversed(range(L)):
        top = l == L - 1
        for m in range(M):
            e = g_all[m].astype(F32) if top else e_one[m]
            d_str[0, m, 0:T, :] = rounded(e * filtered[l, m])
            d_fil[:, m * W:(m + 1) * W] = (e * query[l, m]).astype(BF16)
        d_hat[...] = mm(fw[0], d_fil[...]) + mm(fw[1], d_fil[...])

        def long_gradient():
            re, im = None, None
            for m in range(M):
                dr, di = d_hat[0:H, m * W:(m + 1) * W], d_hat[H:N, m * W:(m + 1) * W]
                mr, mi = m_hat[l, 0:H, m * W:(m + 1) * W], m_hat[l, H:N, m * W:(m + 1) * W]
                a, b = dr * mr + di * mi, di * mr - dr * mi
                re, im = (a, b) if re is None else (re + a, im + b)
            taps_grad = mm3(iv[0, 0:KL, :], iv[1, 0:KL, :], jnp.concatenate([re, im], axis=0))
            fresh[3 * KS:3 * KS + KL, :] = taps_grad
            fresh[3 * KS + KL:3 * KS + KL + 1, :] = taps_grad[0:1]
            fresh_out[l, early_low:early_high, :] = fresh[early_low:early_high, :].astype(BF16)
            send_rows(l, 0, early_low, early_high)

        if not top:
            long_gradient()
        pieces = []
        for m in range(M):
            fr, fi = f_hat[l, 0:H, :], f_hat[l, H:N, :]
            dr, di = d_hat[0:H, m * W:(m + 1) * W], d_hat[H:N, m * W:(m + 1) * W]
            pieces.append(jnp.concatenate([fr * dr + fi * di, fr * di - fi * dr], axis=0))
        d_mix = mm3(iv[0], iv[1], jnp.concatenate(pieces, axis=1))
        for m in range(M):
            d_mix_m = d_mix[:, m * W:(m + 1) * W]
            d_str[1, m, 0:T, :] = rounded(d_mix_m * value[l, m])
            d_str[2, m, 0:T, :] = rounded(d_mix_m * key[l, m])
        taps = [[sf[l, i * KS + j] for j in range(KS)] for i in range(3)]
        for m in range(M):
            def normed_chunk(t):
                total = None
                for i in range(3):
                    for j in range(KS):
                        term = taps[i][j] * d_str[i, m, pl.ds(t + j, CHUNK), :]
                        total = term if total is None else total + term
                d_nor[m, pl.ds(t, CHUNK), :] = total

            chunks(normed_chunk)
        gain = ng[l]
        if l > 0:
            exchange(stages, lambda m: gain * d_nor[m] * xf[l, m])
        if top:
            long_gradient()
        fold = lambda v: jnp.sum(v.reshape(CHUNK // 8, 8, W), axis=0)
        zeros = tuple(jnp.zeros((8, W), F32) for _ in range(3 * KS + 1))

        def grad_chunk(i, carry):
            t = pl.multiple_of(i * CHUNK, CHUNK)
            sums = list(carry)
            for m in range(M):
                streams = [d_str[k, m, pl.ds(t, CHUNK), :] for k in range(3)]
                for j in range(KS):
                    shifted_rows = normed[l, m, pl.ds(t + PAD - j, CHUNK), :]
                    for k in range(3):
                        sums[k * KS + j] = sums[k * KS + j] + fold(streams[k] * shifted_rows)
                gain_terms = d_nor[m, pl.ds(t, CHUNK), :] * xf[l, m, pl.ds(t, CHUNK), :] * scale[l, m, pl.ds(t, CHUNK), :]
                sums[3 * KS] = sums[3 * KS] + fold(gain_terms)
            return tuple(sums)

        sums = lax.fori_loop(0, T // CHUNK, grad_chunk, zeros)
        for row in range(3 * KS):
            fresh[row:row + 1, :] = jnp.sum(sums[row], axis=0, keepdims=True)
        fresh[rows_total - 1:rows_total, :] = jnp.sum(sums[3 * KS], axis=0, keepdims=True)
        for index in (1, 2):
            low, high = spans[index]
            fresh_out[l, low:high, :] = fresh[low:high, :].astype(BF16)
            send_rows(l, index, low, high)
        if l > 0:
            norm_row = exchanged(stages) / D
            for m in range(M):
                term = as_columns(norm_row[:, m * T:(m + 1) * T], W)
                r = scale[l, m]
                e_one[m] = rounded(g_all[m].astype(F32) + r * gain * d_nor[m] - xf[l, m] * (r * r * r) * term)

    for index, (low, high) in enumerate(spans):
        for slot in range(slots):
            @pl.when(own != slot)
            def _():
                remote(fresh_out.at[0, low:high, :], arrived.at[slot, low:high, :], o_send.at[0, index, 0],
                       o_recv.at[index, slot], at(s, q, c)).wait_recv()
                place(slot, low, high, arrived[slot, low:high, :].astype(F32))
    for l in range(L):
        for seq in range(Q):
            here = jnp.logical_and(s == l, q == seq)

            @pl.when(jnp.logical_not(here))
            def _():
                for index, (low, high) in enumerate(spans):
                    remote(fresh_out.at[l, low:high, :], arrived.at[own, low:high, :], o_send.at[l, index, seq],
                           o_recv.at[index, own], at(l, seq, c)).wait_send()
    for copy in x_copies + g_copies:
        copy.wait_send()

    def p0_sent(offset, carry):
        p0_copy(offset).wait_send()
        return carry

    lax.fori_loop(1, Q * C, p0_sent, 0)
    for stage in range(L):
        def sent(offset, carry):
            p, where = peer(offset)
            remote(part_out.at[stage], part.at[stage, me], p_send.at[stage, p], p_recv.at[stage, me], where).wait_send()
            return carry

        lax.fori_loop(1, P_ALL, sent, 0)


def kernel_fits(mesh, args):
    x, sf, lf = args[0], args[2], args[3]
    S, Q = mesh.shape["section"], mesh.shape["seq"]
    width = x.shape[2] // (S * Q)
    rows = Q * x.shape[1]
    return (S == 2 and sf.shape[0] == 1 and width * S * Q == x.shape[2] and width == 128
            and x.shape[1] % CHUNK == 0 and x.shape[0] * x.shape[1] == 128 and sf.shape[2] <= PAD
            and lf.shape[1] % 128 == 0 and lf.shape[1] <= rows)


def by_channels(mesh, x, g, sf, lf, sk, ng):
    S, Q, C = mesh.shape["section"], mesh.shape["seq"], mesh.shape["chan"]
    M, R, channels = x.shape
    KS, KL = sf.shape[2], lf.shape[1]
    W, T, L, G = channels // (S * Q), Q * R, S, S * Q * C
    N = spectrum_size(T, KL)
    fw, iv = spectrum_tables(T, KL)
    rows_total = 3 * KS + KL + 2
    rows_out = -(-rows_total // 16) * 16
    V, dma = pltpu.VMEM, pltpu.SemaphoreType.DMA
    sizes = (S, Q, C, M, R, W, KS, KL, D)
    big = lambda: V((L, M, T, W), F32)
    spans = 3
    result = pl.pallas_call(
        functools.partial(channel_kernel, sizes),
        out_shape=jax.ShapeDtypeStruct((rows_total * S * Q, W), F32),
        in_specs=[pl.BlockSpec(memory_space=pltpu.HBM)] * 8,
        out_specs=pl.BlockSpec(memory_space=pltpu.VMEM),
        scratch_shapes=[
            V((M, R, channels), BF16), V((M, T, W), BF16), V((M, T, W), BF16),
            V((L, 3 * KS, 1, W), F32), V((L, KL, W), F32), V((L, 1, W), F32), V((L, 1, W), F32),
            V(fw.shape, BF16), V(iv.shape, BF16),
            V((1, M * R), F32), V((Q * C, 1, M * R), F32), V((L, 1, M * T), F32), V((L, G, 1, M * T), F32),
            big(), big(), V((L, M, PAD + T, W), F32), big(), big(), big(),
            V((T, M * W), BF16), V((L, N, M * W), F32), big(), V((L, N, W), F32),
            V((T, M * W), BF16), V((N, M * W), F32), V((3, M, T + PAD, W), F32), V((M, T, W), F32),
            V((M, T, W), F32), V((rows_out, W), F32), V((L, rows_out, W), BF16), V((S * Q, rows_out, W), BF16),
            dma((9,)), dma((2, Q)), dma((2, Q)), dma((4,)), dma((4,)), dma((Q * C,)), dma((Q * C,)),
            dma((L, G)), dma((L, G)), dma((L, spans, Q)), dma((spans, S * Q)),
        ],
        compiler_params=pltpu.CompilerParams(collective_id=0, has_side_effects=True, vmem_limit_bytes=60 * 1024 * 1024),
    )(x, g, sf.reshape(3 * KS, 1, channels), lf, sk, ng, jnp.asarray(fw), jnp.asarray(iv))
    return result.reshape(1, rows_total, channels)


def solution(mesh):
    placed = (
        P(None, "seq", "chan"),
        P(None, "seq", "chan"),
        P("section", None, None, "chan"),
        P("section", None, "chan"),
        P("section", "chan"),
        P("section", "chan"),
    )

    def body(*args):
        if kernel_fits(mesh, args):
            return by_channels(mesh, *args)
        return on_device(*args)

    return jax.shard_map(
        body, mesh=mesh, in_specs=placed, out_specs=P("section", None, "chan"), check_vma=False
    )
```

```python
import functools

import jax
import jax.numpy as jnp
import numpy as np
from jax import lax
from jax.experimental import pallas as pl
from jax.experimental.pallas import tpu as pltpu
from jax.sharding import PartitionSpec as P

D = 4096


EPSILON = 1e-06


def shifted(block, axis, distance):
    devices = range(lax.axis_size(axis))
    route = [(i - distance, i) for i in devices if i - distance in devices]
    return lax.ppermute(block, axis, route)


def as_sent(array):
    return jax.tree.map(lambda a: a.astype(jnp.bfloat16) if a.dtype == jnp.float32 else a, array)


def correlate(signal, filters):
    result = lax.conv_general_dilated(
        signal[None],
        filters[:, None, :],
        (1,),
        "VALID",
        dimension_numbers=("NWC", "WIO", "NWC"),
        feature_group_count=signal.shape[1],
        precision=lax.Precision.HIGHEST,
    )
    return result[0]


def rows_before(source_rows, wanted, sender):
    row_count = source_rows.shape[0]
    hop_count = (wanted + row_count - 1) // row_count
    pieces = []
    for distance in range(hop_count, 0, -1):
        taking = min(row_count, wanted - (distance - 1) * row_count)
        pieces.append(sender(source_rows[row_count - taking :], distance))
    return jnp.concatenate(pieces, axis=0)


def rows_after(source_rows, wanted, sender):
    row_count = source_rows.shape[0]
    hop_count = (wanted + row_count - 1) // row_count
    pieces = []
    for distance in range(1, hop_count + 1):
        taking = min(row_count, wanted - (distance - 1) * row_count)
        pieces.append(sender(source_rows[:taking], distance))
    return jnp.concatenate(pieces, axis=0)


def forward_layer(x_rows, short_taps, long_taps, skip_row, gain_row):
    short_len = short_taps.shape[1]
    long_len = long_taps.shape[0]
    x_float = x_rows.astype(jnp.float32)
    squares = lax.psum(jnp.sum(x_float * x_float, axis=1), "chan")
    scale = lax.rsqrt(squares / D + EPSILON)
    normed = (x_float * scale[:, None] * gain_row).astype(jnp.bfloat16)
    h_before = rows_before(
        normed, short_len - 1, lambda shard_rows, distance: shifted(shard_rows, "seq", distance)
    )
    h_extended = jnp.concatenate([h_before, normed], axis=0)
    h_float = h_extended.astype(jnp.float32)
    query = correlate(h_float, short_taps[0][::-1])
    key_rows = correlate(h_float, short_taps[1][::-1])
    value_rows = correlate(h_float, short_taps[2][::-1])
    mixed = (key_rows * value_rows).astype(jnp.bfloat16)
    z_before = rows_before(
        mixed,
        long_len - 1,
        lambda shard_rows, distance: jax.tree.map(
            lambda part, own: part.astype(own.dtype),
            shifted(as_sent(shard_rows), "seq", distance),
            shard_rows,
        ),
    )
    z_extended = jnp.concatenate([z_before, mixed], axis=0)
    mixed_float = z_extended.astype(jnp.float32)
    filtered = correlate(mixed_float, long_taps[::-1]) + skip_row * mixed_float[long_len - 1 :]
    x_next = (x_float + query * filtered).astype(jnp.bfloat16)
    return (x_next, (x_rows, h_extended, z_extended, scale))


def backward_layer(e_rows, stored, short_taps, long_taps, skip_row, gain_row):
    short_len = short_taps.shape[1]
    long_len = long_taps.shape[0]
    x_bf, h_bf, z_bf, scale = stored
    row_count = x_bf.shape[0]
    x_float = x_bf.astype(jnp.float32)
    h_float = h_bf.astype(jnp.float32)
    z_float = z_bf.astype(jnp.float32)
    query = correlate(h_float, short_taps[0][::-1])
    key_rows = correlate(h_float, short_taps[1][::-1])
    value_rows = correlate(h_float, short_taps[2][::-1])
    mixed_float = z_float[long_len - 1 :]
    filtered = correlate(z_float, long_taps[::-1]) + skip_row * mixed_float
    e_float = e_rows.astype(jnp.float32)
    d_query = (e_float * filtered).astype(jnp.bfloat16)
    d_filtered = (e_float * query).astype(jnp.bfloat16)
    filtered_after = rows_after(
        d_filtered, long_len - 1, lambda shard_rows, distance: shifted(shard_rows, "seq", -distance)
    )
    filtered_float = jnp.concatenate([d_filtered, filtered_after], axis=0).astype(jnp.float32)
    d_mixed = correlate(filtered_float, long_taps) + skip_row * filtered_float[:row_count]
    d_key = (d_mixed * value_rows).astype(jnp.bfloat16)
    d_value = (d_mixed * key_rows).astype(jnp.bfloat16)
    streams = jnp.stack([d_query, d_key, d_value], axis=1)
    streams_after = rows_after(
        streams, short_len - 1, lambda shard_rows, distance: shifted(shard_rows, "seq", -distance)
    )
    streams_float = jnp.concatenate([streams, streams_after], axis=0).astype(jnp.float32)
    d_normed = correlate(streams_float[:, 0], short_taps[0])
    d_normed = d_normed + correlate(streams_float[:, 1], short_taps[1])
    d_normed = d_normed + correlate(streams_float[:, 2], short_taps[2])
    fresh = jnp.concatenate(
        [
            correlate(h_float, streams_float[:row_count, 0])[::-1],
            correlate(h_float, streams_float[:row_count, 1])[::-1],
            correlate(h_float, streams_float[:row_count, 2])[::-1],
            correlate(z_float, filtered_float[:row_count])[::-1],
            jnp.sum(filtered_float[:row_count] * mixed_float, axis=0)[None],
            jnp.sum(d_normed * x_float * scale[:, None], axis=0)[None],
        ],
        axis=0,
    )
    norm_term = lax.psum(jnp.sum(gain_row * d_normed * x_float, axis=1), "chan") / D
    e_prev = (
        e_float
        + scale[:, None] * gain_row * d_normed
        - x_float * (scale * scale * scale)[:, None] * norm_term[:, None]
    ).astype(jnp.bfloat16)
    return (e_prev, fresh)


def on_device(inputs, out_grad, short_filters, long_filters, skip_gain, norm_gain):
    sections = lax.axis_size("section")
    section_index = lax.axis_index("section")
    micro_count, row_count, channels = inputs.shape
    short_len = short_filters.shape[2]
    long_len = long_filters.shape[1]
    param_rows = 3 * short_len + long_len + 2
    gathered = (
        lax.all_gather(short_filters, "section", axis=0, tiled=True),
        lax.all_gather(long_filters, "section", axis=0, tiled=True),
        lax.all_gather(skip_gain, "section", axis=0, tiled=True),
        lax.all_gather(norm_gain, "section", axis=0, tiled=True),
    )
    layer_count = gathered[0].shape[0]
    per_device = micro_count // sections
    own_inputs = lax.dynamic_slice_in_dim(inputs, section_index * per_device, per_device, 0)
    own_grads = lax.dynamic_slice_in_dim(out_grad, section_index * per_device, per_device, 0)

    def one_micro(grad_total, micro_rows):
        first_rows, top_grad = micro_rows

        def forward_pass(x_rows, params):
            return forward_layer(x_rows, params[0], params[1], params[2], params[3])

        x_final, stored_all = lax.scan(forward_pass, first_rows, gathered)

        def backward_pass(e_rows, layer_items):
            params, stored = layer_items
            return backward_layer(e_rows, stored, params[0], params[1], params[2], params[3])

        e_first, fresh_all = lax.scan(backward_pass, top_grad, (gathered, stored_all), reverse=True)
        return (grad_total + fresh_all, None)

    grads_start = jnp.zeros((layer_count, param_rows, channels), jnp.float32)
    grads_done, unused_micro = lax.scan(one_micro, grads_start, (own_inputs, own_grads))
    local_grads = lax.psum_scatter(grads_done, "section", scatter_dimension=0, tiled=True)
    return lax.psum(local_grads, "seq")


F32, BF16 = jnp.float32, jnp.bfloat16
PAD = 8
CHUNK = 32


def split(value):
    high = value.astype(BF16)
    return high, (value - high.astype(F32)).astype(BF16)


def mm(a, b):
    return jnp.dot(a, b, preferred_element_type=F32)


def mm3(a_high, a_low, value):
    high, low = split(value)
    return mm(a_high, high) + (mm(a_high, low) + mm(a_low, high))


def lane_sums(value):
    high, low = split(value)
    both = jnp.concatenate([high, low], axis=1)
    ones = jnp.ones((16, both.shape[1]), BF16)
    sums = lax.dot_general(ones, both, (((1,), (1,)), ((), ())), preferred_element_type=F32)
    return sums[0:1]


def as_columns(row, width):
    return jnp.transpose(jnp.broadcast_to(row, (width, row.shape[1])))


def spectrum_size(rows, taps):
    return -(-(rows + taps) // 128) * 128


def spectrum_tables(rows, taps):
    size = spectrum_size(rows, taps)
    angle = (2 * np.pi / size) * (np.arange(size // 2)[:, None] + 0.5) * np.arange(rows)[None]
    forward = np.concatenate([np.cos(angle), -np.sin(angle)], axis=0)
    inverse = (2.0 / size) * forward.T

    def pair(table):
        table = table.astype(np.float32)
        high = table.astype(BF16)
        low = (table - high.astype(np.float32)).astype(BF16)
        return np.stack([high, low])

    return pair(forward), pair(inverse)


def channel_kernel(sizes, x_in, g_in, sf_in, lf_in, sk_in, ng_in, fw_in, iv_in, out,
                   x_own, x_all, g_all, sf, lf, sk, ng, fw, iv,
                   part0_out, part0, part_out, part, xf, scale, normed, query, key, value, mixed, m_hat,
                   filtered, f_hat, d_fil, d_hat, d_str, d_nor, e_one, fresh, fresh_out, arrived,
                   loc_sem, x_send, x_recv, f_send, f_recv, p0_send, p0_recv, p_send, p_recv, o_send, o_recv):
    S, Q, C, M, R, W, KS, KL, D = sizes
    T = Q * R
    N = spectrum_size(T, KL)
    H = N // 2
    L = S
    P_ALL = S * Q * C
    STAGES = 2 * (L - 1)
    s, q, c = lax.axis_index("section"), lax.axis_index("seq"), lax.axis_index("chan")
    me = (s * Q + q) * C + c
    lane = lambda slot: pl.ds(pl.multiple_of(slot * W, W), W)
    rows_at = lambda seq: pl.ds(pl.multiple_of(seq * R, R), R)

    def at(section, seq, chan):
        return {"section": section, "seq": seq, "chan": chan}

    def peer(offset):
        p = lax.rem(me + offset, P_ALL)
        return p, at(p // (Q * C), (p // C) % Q, p % C)

    def remote(src, dst, send, recv, where):
        return pltpu.make_async_remote_copy(src_ref=src, dst_ref=dst, send_sem=send, recv_sem=recv,
                                            device_id=where, device_id_type=pl.DeviceIdType.MESH)

    barrier = pltpu.get_barrier_semaphore()
    for offset in range(1, P_ALL):
        pl.semaphore_signal(barrier, inc=1, device_id=peer(offset)[1], device_id_type=pl.DeviceIdType.MESH)

    own = q * S + s
    locals_ = [
        (x_in, x_own), (x_in.at[:, :, lane(own)], x_all.at[:, rows_at(q), :]),
        (g_in.at[:, :, lane(own)], g_all.at[:, rows_at(q), :]),
        (sf_in.at[:, :, lane(own)], sf.at[s]), (lf_in.at[:, :, lane(own)], lf.at[pl.ds(s, 1)]),
        (sk_in.at[:, lane(own)], sk.at[s]), (ng_in.at[:, lane(own)], ng.at[s]),
        (fw_in, fw), (iv_in, iv),
    ]
    local_copies = [pltpu.make_async_copy(a, b, loc_sem.at[i]) for i, (a, b) in enumerate(locals_)]
    for copy in local_copies:
        copy.start()

    local_copies[0].wait()
    for m in range(M):
        total = None
        for b in range(x_own.shape[2] // W):
            piece = x_own[m, :, b * W:(b + 1) * W].astype(F32)
            total = piece * piece if total is None else total + piece * piece
        d_nor[m, 0:R, :] = total
    gathered = jnp.concatenate([d_nor[m, 0:R, :] for m in range(M)], axis=0)
    part0_out[...] = lane_sums(gathered)

    pl.semaphore_wait(barrier, P_ALL - 1)

    def p0_slot(seq, chan):
        return seq * C + chan

    def p0_copy(offset):
        p = lax.rem(q * C + c + offset, Q * C)
        return remote(part0_out, part0.at[q * C + c], p0_send.at[p], p0_recv.at[q * C + c], at(s, p // C, p % C))

    for offset in range(1, Q * C):
        p0_copy(offset).start()
    x_copies, g_copies = [], []
    for offset in range(1, Q):
        to = lax.rem(q + offset, Q)
        src_slot = to * S + s
        x_copies.append(remote(x_in.at[:, :, lane(src_slot)], x_all.at[:, rows_at(q), :], x_send.at[0, offset], x_recv.at[0, offset], at(s, to, c)))
        g_copies.append(remote(g_in.at[:, :, lane(src_slot)], g_all.at[:, rows_at(q), :], x_send.at[1, offset], x_recv.at[1, offset], at(s, to, c)))
    for copy in x_copies:
        copy.start()
    mate = 1 - s
    theirs = q * S + mate
    f_copies = [
        remote(src, dst, f_send.at[i], f_recv.at[i], at(mate, q, c))
        for i, (src, dst) in enumerate([
            (sf_in.at[:, :, lane(theirs)], sf.at[s]), (lf_in.at[:, :, lane(theirs)], lf.at[pl.ds(s, 1)]),
            (sk_in.at[:, lane(theirs)], sk.at[s]), (ng_in.at[:, lane(theirs)], ng.at[s]),
        ])
    ]
    for copy in f_copies:
        copy.start()
    for copy in g_copies:
        copy.start()

    for l in range(L):
        for m in range(M):
            normed[l, m, 0:PAD, :] = jnp.zeros((PAD, W), F32)
    for i in range(3):
        for m in range(M):
            d_str[i, m, T:T + PAD, :] = jnp.zeros((PAD, W), F32)
    for copy in local_copies[1:]:
        copy.wait()
    for copy in f_copies:
        copy.wait()
    for l in range(L):
        f_hat[l] = mm3(fw[0, :, 0:KL], fw[1, :, 0:KL], lf[l])
        f_hat[l, 0:H, :] = f_hat[l, 0:H, :] + sk[l]

    part0[q * C + c] = part0_out[...]
    for offset in range(1, Q * C):
        p = lax.rem(q * C + c + offset, Q * C)
        remote(part0_out, part0.at[p], p0_send.at[p], p0_recv.at[p], at(s, p // C, p % C)).wait_recv()
    for seq in range(Q):
        row = part0[seq * C]
        for chan in range(1, C):
            row = row + part0[seq * C + chan]
        columns = as_columns(lax.rsqrt(row / D + EPSILON), W)
        for m in range(M):
            scale[0, m, seq * R:(seq + 1) * R, :] = columns[m * R:(m + 1) * R]
    for copy in x_copies:
        copy.wait_recv()
    for m in range(M):
        for t in range(0, T, R):
            xf[0, m, t:t + R, :] = x_all[m, t:t + R, :].astype(F32)

    def chunks(body):
        def step(i, carry):
            body(pl.multiple_of(i * CHUNK, CHUNK))
            return carry

        lax.fori_loop(0, T // CHUNK, step, 0)

    def rounded(v):
        return v.astype(BF16).astype(F32)

    def lanes(m):
        return slice(m * W, (m + 1) * W)

    def inverse(product):
        high, low = split(product)
        both = mm(iv[0], jnp.concatenate([high, low], axis=1))
        return both[:, 0:W] + (both[:, W:2 * W] + mm(iv[1], high))

    def forward(l, m):
        gain = ng[l]

        def norm_chunk(t):
            v = xf[l, m, pl.ds(t, CHUNK), :] * scale[l, m, pl.ds(t, CHUNK), :] * gain
            normed[l, m, pl.ds(t + PAD, CHUNK), :] = rounded(v)

        chunks(norm_chunk)
        taps = [[sf[l, i * KS + j] for j in range(KS)] for i in range(3)]

        def short_chunk(t):
            sums = [None] * 3
            for j in range(KS):
                shifted_rows = normed[l, m, pl.ds(t + PAD - j, CHUNK), :]
                for i in range(3):
                    term = taps[i][j] * shifted_rows
                    sums[i] = term if sums[i] is None else sums[i] + term
            query[l, m, pl.ds(t, CHUNK), :] = sums[0]
            key[l, m, pl.ds(t, CHUNK), :] = sums[1]
            value[l, m, pl.ds(t, CHUNK), :] = sums[2]
            mixed[pl.ds(t, CHUNK), lanes(m)] = (sums[1] * sums[2]).astype(BF16)

        chunks(short_chunk)
        m_hat[l, :, lanes(m)] = mm(fw[0], mixed[:, lanes(m)]) + mm(fw[1], mixed[:, lanes(m)])
        fr, fi = f_hat[l, 0:H, :], f_hat[l, H:N, :]
        mr, mi = m_hat[l, 0:H, lanes(m)], m_hat[l, H:N, lanes(m)]
        filtered[l, m] = inverse(jnp.concatenate([fr * mr - fi * mi, fr * mi + fi * mr], axis=0))

    def exchange(stage, m, rows):
        i = stage * M + m
        part_out[i] = lane_sums(rows)
        for offset in range(1, P_ALL):
            p, where = peer(offset)
            remote(part_out.at[i], part.at[i, me], p_send.at[i, p], p_recv.at[i, me], where).start()

    def exchanged(stage, m):
        i = stage * M + m
        part[i, me] = part_out[i]
        for offset in range(1, P_ALL):
            p, where = peer(offset)
            remote(part_out.at[i], part.at[i, p], p_send.at[i, p], p_recv.at[i, p], where).wait_recv()
        rows = [part[i, p] for p in range(P_ALL)]
        while len(rows) > 1:
            rows = [a + b for a, b in zip(rows[::2], rows[1::2])] + ([rows[-1]] if len(rows) % 2 else [])
        return rows[0]

    def forward_and_on(l, m):
        forward(l, m)
        if l < L - 1:
            xf[l + 1, m] = rounded(xf[l, m] + query[l, m] * filtered[l, m])
            exchange(l, m, xf[l + 1, m] * xf[l + 1, m])

    slots = S * Q
    rows_total = 3 * KS + KL + 2

    def place(slot, low, high, values):
        high = min(high, rows_total)
        out[pl.ds(low * slots + slot, high - low, stride=slots), :] = values[0:high - low]

    def send_rows(l, part_index, low, high):
        for seq in range(Q):
            here = jnp.logical_and(s == l, q == seq)

            @pl.when(here)
            def _():
                place(own, low, high, fresh[low:high, :])

            @pl.when(jnp.logical_not(here))
            def _():
                remote(fresh_out.at[l, low:high, :], arrived.at[own, low:high, :], o_send.at[l, part_index, seq],
                       o_recv.at[part_index, own], at(l, seq, c)).start()

    early_low = -(-3 * KS // 16) * 16
    early_high = (3 * KS + KL) // 16 * 16
    late_high = fresh_out.shape[1]
    spans = [(early_low, early_high), (0, early_low), (early_high, late_high)]

    def cotangent(l, m):
        return g_all[m].astype(F32) if l == L - 1 else e_one[l, m]

    def backward_filtered(l, m):
        e = cotangent(l, m)
        d_str[0, m, 0:T, :] = rounded(e * filtered[l, m])
        d_fil[:, lanes(m)] = (e * query[l, m]).astype(BF16)
        d_hat[:, lanes(m)] = mm(fw[0], d_fil[:, lanes(m)]) + mm(fw[1], d_fil[:, lanes(m)])

    def backward_normed(l, m):
        fr, fi = f_hat[l, 0:H, :], f_hat[l, H:N, :]
        dr, di = d_hat[0:H, lanes(m)], d_hat[H:N, lanes(m)]
        d_mix = inverse(jnp.concatenate([fr * dr + fi * di, fr * di - fi * dr], axis=0))
        d_str[1, m, 0:T, :] = rounded(d_mix * value[l, m])
        d_str[2, m, 0:T, :] = rounded(d_mix * key[l, m])
        taps = [[sf[l, i * KS + j] for j in range(KS)] for i in range(3)]

        def normed_chunk(t):
            total = None
            for i in range(3):
                for j in range(KS):
                    term = taps[i][j] * d_str[i, m, pl.ds(t + j, CHUNK), :]
                    total = term if total is None else total + term
            d_nor[m, pl.ds(t, CHUNK), :] = total

        chunks(normed_chunk)

    def long_gradient(l):
        re, im = None, None
        for m in range(M):
            dr, di = d_hat[0:H, lanes(m)], d_hat[H:N, lanes(m)]
            mr, mi = m_hat[l, 0:H, lanes(m)], m_hat[l, H:N, lanes(m)]
            a, b = dr * mr + di * mi, di * mr - dr * mi
            re, im = (a, b) if re is None else (re + a, im + b)
        taps_grad = mm3(iv[0, 0:KL, :], iv[1, 0:KL, :], jnp.concatenate([re, im], axis=0))
        fresh[3 * KS:3 * KS + KL, :] = taps_grad
        fresh[3 * KS + KL:3 * KS + KL + 1, :] = taps_grad[0:1]
        fresh_out[l, early_low:early_high, :] = fresh[early_low:early_high, :].astype(BF16)
        send_rows(l, 0, early_low, early_high)

    def short_gradients(l):
        fold = lambda v: jnp.sum(v.reshape(CHUNK // 8, 8, W), axis=0)
        zeros = tuple(jnp.zeros((8, W), F32) for _ in range(3 * KS + 1))

        def grad_chunk(i, carry):
            t = pl.multiple_of(i * CHUNK, CHUNK)
            sums = list(carry)
            for m in range(M):
                streams = [d_str[k, m, pl.ds(t, CHUNK), :] for k in range(3)]
                for j in range(KS):
                    shifted_rows = normed[l, m, pl.ds(t + PAD - j, CHUNK), :]
                    for k in range(3):
                        sums[k * KS + j] = sums[k * KS + j] + fold(streams[k] * shifted_rows)
                gain_terms = d_nor[m, pl.ds(t, CHUNK), :] * xf[l, m, pl.ds(t, CHUNK), :] * scale[l, m, pl.ds(t, CHUNK), :]
                sums[3 * KS] = sums[3 * KS] + fold(gain_terms)
            return tuple(sums)

        sums = lax.fori_loop(0, T // CHUNK, grad_chunk, zeros)
        for row in range(3 * KS):
            fresh[row:row + 1, :] = jnp.sum(sums[row], axis=0, keepdims=True)
        fresh[rows_total - 1:rows_total, :] = jnp.sum(sums[3 * KS], axis=0, keepdims=True)
        for index in (1, 2):
            low, high = spans[index]
            fresh_out[l, low:high, :] = fresh[low:high, :].astype(BF16)
            send_rows(l, index, low, high)

    for l in range(L - 1):
        for m in range(M):
            if l > 0:
                scale[l, m] = as_columns(lax.rsqrt(exchanged(l - 1, m) / D + EPSILON), W)
            forward_and_on(l, m)
    top = L - 1
    for copy in g_copies:
        copy.wait_recv()
    for m in range(M):
        scale[top, m] = as_columns(lax.rsqrt(exchanged(top - 1, m) / D + EPSILON), W)
        forward(top, m)
        backward_filtered(top, m)
        backward_normed(top, m)
        exchange(top, m, ng[top] * d_nor[m] * xf[top, m])
    long_gradient(top)
    for l in reversed(range(L)):
        short_gradients(l)
        if l > 0:
            stage = 2 * top - l
            below = l - 1
            for m in range(M):
                term = as_columns(exchanged(stage, m) / D, W)
                r = scale[l, m]
                e_one[below, m] = rounded(cotangent(l, m) + r * ng[l] * d_nor[m] - xf[l, m] * (r * r * r) * term)
                backward_filtered(below, m)
                if m == M - 1:
                    long_gradient(below)
                backward_normed(below, m)
                if below > 0:
                    exchange(stage + 1, m, ng[below] * d_nor[m] * xf[below, m])

    for index, (low, high) in enumerate(spans):
        for slot in range(slots):
            @pl.when(own != slot)
            def _():
                remote(fresh_out.at[0, low:high, :], arrived.at[slot, low:high, :], o_send.at[0, index, 0],
                       o_recv.at[index, slot], at(s, q, c)).wait_recv()
                place(slot, low, high, arrived[slot, low:high, :].astype(F32))
    for l in range(L):
        for seq in range(Q):
            here = jnp.logical_and(s == l, q == seq)

            @pl.when(jnp.logical_not(here))
            def _():
                for index, (low, high) in enumerate(spans):
                    remote(fresh_out.at[l, low:high, :], arrived.at[own, low:high, :], o_send.at[l, index, seq],
                           o_recv.at[index, own], at(l, seq, c)).wait_send()
    for copy in x_copies + g_copies:
        copy.wait_send()

    def p0_sent(offset, carry):
        p0_copy(offset).wait_send()
        return carry

    lax.fori_loop(1, Q * C, p0_sent, 0)
    for stage in range(STAGES * M):
        def sent(offset, carry):
            p, where = peer(offset)
            remote(part_out.at[stage], part.at[stage, me], p_send.at[stage, p], p_recv.at[stage, me], where).wait_send()
            return carry

        lax.fori_loop(1, P_ALL, sent, 0)


def kernel_fits(mesh, args):
    x, sf, lf = args[0], args[2], args[3]
    S, Q = mesh.shape["section"], mesh.shape["seq"]
    width = x.shape[2] // (S * Q)
    rows = Q * x.shape[1]
    return (S == 2 and sf.shape[0] == 1 and width * S * Q == x.shape[2] and width == 128
            and x.shape[1] % CHUNK == 0 and x.shape[0] * x.shape[1] == 128 and sf.shape[2] <= PAD
            and lf.shape[1] % 128 == 0 and lf.shape[1] <= rows)


def by_channels(mesh, x, g, sf, lf, sk, ng):
    S, Q, C = mesh.shape["section"], mesh.shape["seq"], mesh.shape["chan"]
    M, R, channels = x.shape
    KS, KL = sf.shape[2], lf.shape[1]
    W, T, L, G = channels // (S * Q), Q * R, S, S * Q * C
    N = spectrum_size(T, KL)
    fw, iv = spectrum_tables(T, KL)
    rows_total = 3 * KS + KL + 2
    rows_out = -(-rows_total // 16) * 16
    V, dma = pltpu.VMEM, pltpu.SemaphoreType.DMA
    sizes = (S, Q, C, M, R, W, KS, KL, D)
    big = lambda: V((L, M, T, W), F32)
    spans = 3
    stages = 2 * (L - 1)
    pinned = [pltpu.with_memory_space_constraint(a, pltpu.HBM) for a in (x, g, sf.reshape(3 * KS, 1, channels), lf, sk, ng, jnp.asarray(fw), jnp.asarray(iv))]
    result = pl.pallas_call(
        functools.partial(channel_kernel, sizes),
        out_shape=jax.ShapeDtypeStruct((rows_total * S * Q, W), F32),
        in_specs=[pl.BlockSpec(memory_space=pltpu.HBM)] * 8,
        out_specs=pl.BlockSpec(memory_space=pltpu.VMEM),
        scratch_shapes=[
            V((M, R, channels), BF16), V((M, T, W), BF16), V((M, T, W), BF16),
            V((L, 3 * KS, 1, W), F32), V((L, KL, W), F32), V((L, 1, W), F32), V((L, 1, W), F32),
            V(fw.shape, BF16), V(iv.shape, BF16),
            V((1, M * R), F32), V((Q * C, 1, M * R), F32), V((stages * M, 1, T), F32), V((stages * M, G, 1, T), F32),
            big(), big(), V((L, M, PAD + T, W), F32), big(), big(), big(),
            V((T, M * W), BF16), V((L, N, M * W), F32), big(), V((L, N, W), F32),
            V((T, M * W), BF16), V((N, M * W), F32), V((3, M, T + PAD, W), F32), V((M, T, W), F32),
            V((L, M, T, W), F32), V((rows_out, W), F32), V((L, rows_out, W), BF16), V((S * Q, rows_out, W), BF16),
            dma((9,)), dma((2, Q)), dma((2, Q)), dma((4,)), dma((4,)), dma((Q * C,)), dma((Q * C,)),
            dma((stages * M, G)), dma((stages * M, G)), dma((L, spans, Q)), dma((spans, S * Q)),
        ],
        compiler_params=pltpu.CompilerParams(collective_id=0, has_side_effects=True, vmem_limit_bytes=40 * 1024 * 1024),
    )(*pinned)
    return result.reshape(1, rows_total, channels)


def solution(mesh):
    placed = (
        P(None, "seq", "chan"),
        P(None, "seq", "chan"),
        P("section", None, None, "chan"),
        P("section", None, "chan"),
        P("section", "chan"),
        P("section", "chan"),
    )

    def body(*args):
        if kernel_fits(mesh, args):
            return by_channels(mesh, *args)
        return on_device(*args)

    return jax.shard_map(
        body, mesh=mesh, in_specs=placed, out_specs=P("section", None, "chan"), check_vma=False
    )
```

```python
import functools

import jax
import jax.numpy as jnp
import numpy as np
from jax import lax
from jax.experimental import pallas as pl
from jax.experimental.pallas import tpu as pltpu
from jax.sharding import PartitionSpec as P

D = 4096


EPSILON = 1e-06


def shifted(block, axis, distance):
    devices = range(lax.axis_size(axis))
    route = [(i - distance, i) for i in devices if i - distance in devices]
    return lax.ppermute(block, axis, route)


def as_sent(array):
    return jax.tree.map(lambda a: a.astype(jnp.bfloat16) if a.dtype == jnp.float32 else a, array)


def correlate(signal, filters):
    result = lax.conv_general_dilated(
        signal[None],
        filters[:, None, :],
        (1,),
        "VALID",
        dimension_numbers=("NWC", "WIO", "NWC"),
        feature_group_count=signal.shape[1],
        precision=lax.Precision.HIGHEST,
    )
    return result[0]


def rows_before(source_rows, wanted, sender):
    row_count = source_rows.shape[0]
    hop_count = (wanted + row_count - 1) // row_count
    pieces = []
    for distance in range(hop_count, 0, -1):
        taking = min(row_count, wanted - (distance - 1) * row_count)
        pieces.append(sender(source_rows[row_count - taking :], distance))
    return jnp.concatenate(pieces, axis=0)


def rows_after(source_rows, wanted, sender):
    row_count = source_rows.shape[0]
    hop_count = (wanted + row_count - 1) // row_count
    pieces = []
    for distance in range(1, hop_count + 1):
        taking = min(row_count, wanted - (distance - 1) * row_count)
        pieces.append(sender(source_rows[:taking], distance))
    return jnp.concatenate(pieces, axis=0)


def forward_layer(x_rows, short_taps, long_taps, skip_row, gain_row):
    short_len = short_taps.shape[1]
    long_len = long_taps.shape[0]
    x_float = x_rows.astype(jnp.float32)
    squares = lax.psum(jnp.sum(x_float * x_float, axis=1), "chan")
    scale = lax.rsqrt(squares / D + EPSILON)
    normed = (x_float * scale[:, None] * gain_row).astype(jnp.bfloat16)
    h_before = rows_before(
        normed, short_len - 1, lambda shard_rows, distance: shifted(shard_rows, "seq", distance)
    )
    h_extended = jnp.concatenate([h_before, normed], axis=0)
    h_float = h_extended.astype(jnp.float32)
    query = correlate(h_float, short_taps[0][::-1])
    key_rows = correlate(h_float, short_taps[1][::-1])
    value_rows = correlate(h_float, short_taps[2][::-1])
    mixed = (key_rows * value_rows).astype(jnp.bfloat16)
    z_before = rows_before(
        mixed,
        long_len - 1,
        lambda shard_rows, distance: jax.tree.map(
            lambda part, own: part.astype(own.dtype),
            shifted(as_sent(shard_rows), "seq", distance),
            shard_rows,
        ),
    )
    z_extended = jnp.concatenate([z_before, mixed], axis=0)
    mixed_float = z_extended.astype(jnp.float32)
    filtered = correlate(mixed_float, long_taps[::-1]) + skip_row * mixed_float[long_len - 1 :]
    x_next = (x_float + query * filtered).astype(jnp.bfloat16)
    return (x_next, (x_rows, h_extended, z_extended, scale))


def backward_layer(e_rows, stored, short_taps, long_taps, skip_row, gain_row):
    short_len = short_taps.shape[1]
    long_len = long_taps.shape[0]
    x_bf, h_bf, z_bf, scale = stored
    row_count = x_bf.shape[0]
    x_float = x_bf.astype(jnp.float32)
    h_float = h_bf.astype(jnp.float32)
    z_float = z_bf.astype(jnp.float32)
    query = correlate(h_float, short_taps[0][::-1])
    key_rows = correlate(h_float, short_taps[1][::-1])
    value_rows = correlate(h_float, short_taps[2][::-1])
    mixed_float = z_float[long_len - 1 :]
    filtered = correlate(z_float, long_taps[::-1]) + skip_row * mixed_float
    e_float = e_rows.astype(jnp.float32)
    d_query = (e_float * filtered).astype(jnp.bfloat16)
    d_filtered = (e_float * query).astype(jnp.bfloat16)
    filtered_after = rows_after(
        d_filtered, long_len - 1, lambda shard_rows, distance: shifted(shard_rows, "seq", -distance)
    )
    filtered_float = jnp.concatenate([d_filtered, filtered_after], axis=0).astype(jnp.float32)
    d_mixed = correlate(filtered_float, long_taps) + skip_row * filtered_float[:row_count]
    d_key = (d_mixed * value_rows).astype(jnp.bfloat16)
    d_value = (d_mixed * key_rows).astype(jnp.bfloat16)
    streams = jnp.stack([d_query, d_key, d_value], axis=1)
    streams_after = rows_after(
        streams, short_len - 1, lambda shard_rows, distance: shifted(shard_rows, "seq", -distance)
    )
    streams_float = jnp.concatenate([streams, streams_after], axis=0).astype(jnp.float32)
    d_normed = correlate(streams_float[:, 0], short_taps[0])
    d_normed = d_normed + correlate(streams_float[:, 1], short_taps[1])
    d_normed = d_normed + correlate(streams_float[:, 2], short_taps[2])
    fresh = jnp.concatenate(
        [
            correlate(h_float, streams_float[:row_count, 0])[::-1],
            correlate(h_float, streams_float[:row_count, 1])[::-1],
            correlate(h_float, streams_float[:row_count, 2])[::-1],
            correlate(z_float, filtered_float[:row_count])[::-1],
            jnp.sum(filtered_float[:row_count] * mixed_float, axis=0)[None],
            jnp.sum(d_normed * x_float * scale[:, None], axis=0)[None],
        ],
        axis=0,
    )
    norm_term = lax.psum(jnp.sum(gain_row * d_normed * x_float, axis=1), "chan") / D
    e_prev = (
        e_float
        + scale[:, None] * gain_row * d_normed
        - x_float * (scale * scale * scale)[:, None] * norm_term[:, None]
    ).astype(jnp.bfloat16)
    return (e_prev, fresh)


def on_device(inputs, out_grad, short_filters, long_filters, skip_gain, norm_gain):
    sections = lax.axis_size("section")
    section_index = lax.axis_index("section")
    micro_count, row_count, channels = inputs.shape
    short_len = short_filters.shape[2]
    long_len = long_filters.shape[1]
    param_rows = 3 * short_len + long_len + 2
    gathered = (
        lax.all_gather(short_filters, "section", axis=0, tiled=True),
        lax.all_gather(long_filters, "section", axis=0, tiled=True),
        lax.all_gather(skip_gain, "section", axis=0, tiled=True),
        lax.all_gather(norm_gain, "section", axis=0, tiled=True),
    )
    layer_count = gathered[0].shape[0]
    per_device = micro_count // sections
    own_inputs = lax.dynamic_slice_in_dim(inputs, section_index * per_device, per_device, 0)
    own_grads = lax.dynamic_slice_in_dim(out_grad, section_index * per_device, per_device, 0)

    def one_micro(grad_total, micro_rows):
        first_rows, top_grad = micro_rows

        def forward_pass(x_rows, params):
            return forward_layer(x_rows, params[0], params[1], params[2], params[3])

        x_final, stored_all = lax.scan(forward_pass, first_rows, gathered)

        def backward_pass(e_rows, layer_items):
            params, stored = layer_items
            return backward_layer(e_rows, stored, params[0], params[1], params[2], params[3])

        e_first, fresh_all = lax.scan(backward_pass, top_grad, (gathered, stored_all), reverse=True)
        return (grad_total + fresh_all, None)

    grads_start = jnp.zeros((layer_count, param_rows, channels), jnp.float32)
    grads_done, unused_micro = lax.scan(one_micro, grads_start, (own_inputs, own_grads))
    local_grads = lax.psum_scatter(grads_done, "section", scatter_dimension=0, tiled=True)
    return lax.psum(local_grads, "seq")


F32, BF16 = jnp.float32, jnp.bfloat16
PAD = 8
CHUNK = 32


def split(value):
    high = value.astype(BF16)
    return high, (value - high.astype(F32)).astype(BF16)


def mm(a, b):
    return jnp.dot(a, b, preferred_element_type=F32)


def mm3(a_high, a_low, value):
    high, low = split(value)
    return mm(a_high, high) + (mm(a_high, low) + mm(a_low, high))


def lane_sums(value):
    high, low = split(value)
    both = jnp.concatenate([high, low], axis=1)
    ones = jnp.ones((16, both.shape[1]), BF16)
    sums = lax.dot_general(ones, both, (((1,), (1,)), ((), ())), preferred_element_type=F32)
    return sums[0:1]


def as_columns(row, width):
    return jnp.transpose(jnp.broadcast_to(row, (width, row.shape[1])))


def spectrum_size(rows, taps):
    return -(-(rows + taps) // 128) * 128


def spectrum_tables(rows, taps):
    size = spectrum_size(rows, taps)
    angle = (2 * np.pi / size) * (np.arange(size // 2)[:, None] + 0.5) * np.arange(rows)[None]
    forward = np.concatenate([np.cos(angle), -np.sin(angle)], axis=0)
    inverse = (2.0 / size) * forward.T

    def pair(table):
        table = table.astype(np.float32)
        high = table.astype(BF16)
        low = (table - high.astype(np.float32)).astype(BF16)
        return np.stack([high, low])

    return pair(forward), pair(inverse)


def channel_kernel(sizes, x_in, g_in, sf_in, lf_in, sk_in, ng_in, fw_in, iv_in, out,
                   x_own, x_all, g_all, sf, lf, sk, ng, fw, iv,
                   part0_out, part0, part_out, part, xf, scale, normed, query, key, value, mixed, m_hat,
                   filtered, f_hat, d_fil, d_hat, d_str, d_nor, e_one, fresh, fresh_out, arrived,
                   loc_sem, x_send, x_recv, f_send, f_recv, p0_send, p0_recv, p_send, p_recv, o_send, o_recv):
    S, Q, C, M, R, W, KS, KL, D = sizes
    T = Q * R
    N = spectrum_size(T, KL)
    H = N // 2
    L = S
    P_ALL = S * Q * C
    STAGES = 2 * (L - 1)
    s, q, c = lax.axis_index("section"), lax.axis_index("seq"), lax.axis_index("chan")
    me = (s * Q + q) * C + c
    lane = lambda slot: pl.ds(pl.multiple_of(slot * W, W), W)
    rows_at = lambda seq: pl.ds(pl.multiple_of(seq * R, R), R)

    def at(section, seq, chan):
        return {"section": section, "seq": seq, "chan": chan}

    def peer(offset):
        p = lax.rem(me + offset, P_ALL)
        return p, at(p // (Q * C), (p // C) % Q, p % C)

    def remote(src, dst, send, recv, where):
        return pltpu.make_async_remote_copy(src_ref=src, dst_ref=dst, send_sem=send, recv_sem=recv,
                                            device_id=where, device_id_type=pl.DeviceIdType.MESH)

    barrier = pltpu.get_barrier_semaphore()
    for offset in range(1, P_ALL):
        pl.semaphore_signal(barrier, inc=1, device_id=peer(offset)[1], device_id_type=pl.DeviceIdType.MESH)

    own = q * S + s
    locals_ = [
        (x_in, x_own), (x_in.at[:, :, lane(own)], x_all.at[:, rows_at(q), :]),
        (g_in.at[:, :, lane(own)], g_all.at[:, rows_at(q), :]),
        (sf_in.at[:, :, lane(own)], sf.at[s]), (lf_in.at[:, :, lane(own)], lf.at[pl.ds(s, 1)]),
        (sk_in.at[:, lane(own)], sk.at[s]), (ng_in.at[:, lane(own)], ng.at[s]),
        (fw_in, fw), (iv_in, iv),
    ]
    local_copies = [pltpu.make_async_copy(a, b, loc_sem.at[i]) for i, (a, b) in enumerate(locals_)]
    for copy in local_copies:
        copy.start()

    local_copies[0].wait()
    for m in range(M):
        total = None
        for b in range(x_own.shape[2] // W):
            piece = x_own[m, :, b * W:(b + 1) * W].astype(F32)
            total = piece * piece if total is None else total + piece * piece
        d_nor[m, 0:R, :] = total
    gathered = jnp.concatenate([d_nor[m, 0:R, :] for m in range(M)], axis=0)
    part0_out[...] = lane_sums(gathered)

    pl.semaphore_wait(barrier, P_ALL - 1)

    def p0_slot(seq, chan):
        return seq * C + chan

    def p0_copy(offset):
        p = lax.rem(q * C + c + offset, Q * C)
        return remote(part0_out, part0.at[q * C + c], p0_send.at[p], p0_recv.at[q * C + c], at(s, p // C, p % C))

    for offset in range(1, Q * C):
        p0_copy(offset).start()
    x_copies, g_copies = [], []
    for offset in range(1, Q):
        to = lax.rem(q + offset, Q)
        src_slot = to * S + s
        for m in range(M):
            x_copies.append((m, remote(x_in.at[m, :, lane(src_slot)], x_all.at[m, rows_at(q), :], x_send.at[m, offset], x_recv.at[m, offset], at(s, to, c))))
        g_copies.append(remote(g_in.at[:, :, lane(src_slot)], g_all.at[:, rows_at(q), :], x_send.at[M, offset], x_recv.at[M, offset], at(s, to, c)))
    x_copies = [[copy for index, copy in x_copies if index == m] for m in range(M)]
    for m in range(M):
        for copy in x_copies[m]:
            copy.start()
    mate = 1 - s
    theirs = q * S + mate
    f_copies = [
        remote(src, dst, f_send.at[i], f_recv.at[i], at(mate, q, c))
        for i, (src, dst) in enumerate([
            (sf_in.at[:, :, lane(theirs)], sf.at[s]), (lf_in.at[:, :, lane(theirs)], lf.at[pl.ds(s, 1)]),
            (sk_in.at[:, lane(theirs)], sk.at[s]), (ng_in.at[:, lane(theirs)], ng.at[s]),
        ])
    ]
    for copy in f_copies:
        copy.start()

    for l in range(L):
        for m in range(M):
            normed[l, m, 0:PAD, :] = jnp.zeros((PAD, W), F32)
    for i in range(3):
        for m in range(M):
            d_str[i, m, T:T + PAD, :] = jnp.zeros((PAD, W), F32)
    for copy in local_copies[1:]:
        copy.wait()
    for copy in f_copies:
        copy.wait()
    for l in range(L):
        f_hat[l] = mm3(fw[0, :, 0:KL], fw[1, :, 0:KL], lf[l])
        f_hat[l, 0:H, :] = f_hat[l, 0:H, :] + sk[l]

    part0[q * C + c] = part0_out[...]
    for offset in range(1, Q * C):
        p = lax.rem(q * C + c + offset, Q * C)
        remote(part0_out, part0.at[p], p0_send.at[p], p0_recv.at[p], at(s, p // C, p % C)).wait_recv()
    for seq in range(Q):
        row = part0[seq * C]
        for chan in range(1, C):
            row = row + part0[seq * C + chan]
        columns = as_columns(lax.rsqrt(row / D + EPSILON), W)
        for m in range(M):
            scale[0, m, seq * R:(seq + 1) * R, :] = columns[m * R:(m + 1) * R]

    def chunks(body):
        def step(i, carry):
            body(pl.multiple_of(i * CHUNK, CHUNK))
            return carry

        lax.fori_loop(0, T // CHUNK, step, 0, unroll=True)

    def rounded(v):
        return v.astype(BF16).astype(F32)

    def lanes(m):
        return slice(m * W, (m + 1) * W)

    def inverse(product):
        high, low = split(product)
        both = mm(iv[0], jnp.concatenate([high, low], axis=1))
        return both[:, 0:W] + (both[:, W:2 * W] + mm(iv[1], high))

    def forward(l, m):
        gain = ng[l]

        def norm_chunk(t):
            v = xf[l, m, pl.ds(t, CHUNK), :] * scale[l, m, pl.ds(t, CHUNK), :] * gain
            normed[l, m, pl.ds(t + PAD, CHUNK), :] = rounded(v)

        chunks(norm_chunk)
        taps = [[sf[l, i * KS + j] for j in range(KS)] for i in range(3)]

        def short_chunk(t):
            sums = [None] * 3
            for j in range(KS):
                shifted_rows = normed[l, m, pl.ds(t + PAD - j, CHUNK), :]
                for i in range(3):
                    term = taps[i][j] * shifted_rows
                    sums[i] = term if sums[i] is None else sums[i] + term
            query[l, m, pl.ds(t, CHUNK), :] = sums[0]
            key[l, m, pl.ds(t, CHUNK), :] = sums[1]
            value[l, m, pl.ds(t, CHUNK), :] = sums[2]
            mixed[pl.ds(t, CHUNK), lanes(m)] = (sums[1] * sums[2]).astype(BF16)

        chunks(short_chunk)
        m_hat[l, :, lanes(m)] = mm(fw[0], mixed[:, lanes(m)]) + mm(fw[1], mixed[:, lanes(m)])
        fr, fi = f_hat[l, 0:H, :], f_hat[l, H:N, :]
        mr, mi = m_hat[l, 0:H, lanes(m)], m_hat[l, H:N, lanes(m)]
        filtered[l, m] = inverse(jnp.concatenate([fr * mr - fi * mi, fr * mi + fi * mr], axis=0))

    def exchange(stage, m, rows):
        i = stage * M + m
        part_out[i] = lane_sums(rows)
        for offset in range(1, P_ALL):
            p, where = peer(offset)
            remote(part_out.at[i], part.at[i, me], p_send.at[i, p], p_recv.at[i, me], where).start()

    def exchanged(stage, m):
        i = stage * M + m
        part[i, me] = part_out[i]
        for offset in range(1, P_ALL):
            p, where = peer(offset)
            remote(part_out.at[i], part.at[i, p], p_send.at[i, p], p_recv.at[i, p], where).wait_recv()
        rows = [part[i, p] for p in range(P_ALL)]
        while len(rows) > 1:
            rows = [a + b for a, b in zip(rows[::2], rows[1::2])] + ([rows[-1]] if len(rows) % 2 else [])
        return rows[0]

    def forward_and_on(l, m):
        forward(l, m)
        if l < L - 1:
            xf[l + 1, m] = rounded(xf[l, m] + query[l, m] * filtered[l, m])
            exchange(l, m, xf[l + 1, m] * xf[l + 1, m])

    slots = S * Q
    rows_total = 3 * KS + KL + 2

    def place(slot, low, high, values):
        high = min(high, rows_total)
        out[pl.ds(low * slots + slot, high - low, stride=slots), :] = values[0:high - low]

    def send_rows(l, part_index, low, high):
        for seq in range(Q):
            here = jnp.logical_and(s == l, q == seq)

            @pl.when(here)
            def _():
                place(own, low, high, fresh[low:high, :])

            @pl.when(jnp.logical_not(here))
            def _():
                remote(fresh_out.at[l, low:high, :], arrived.at[own, low:high, :], o_send.at[l, part_index, seq],
                       o_recv.at[part_index, own], at(l, seq, c)).start()

    early_low = -(-3 * KS // 16) * 16
    early_high = (3 * KS + KL) // 16 * 16
    late_high = fresh_out.shape[1]
    spans = [(early_low, early_high), (0, early_low), (early_high, late_high)]

    def cotangent(l, m):
        return g_all[m].astype(F32) if l == L - 1 else e_one[l, m]

    def backward_filtered(l, m):
        e = cotangent(l, m)
        d_str[0, m, 0:T, :] = rounded(e * filtered[l, m])
        d_fil[:, lanes(m)] = (e * query[l, m]).astype(BF16)
        d_hat[:, lanes(m)] = mm(fw[0], d_fil[:, lanes(m)]) + mm(fw[1], d_fil[:, lanes(m)])

    def backward_normed(l, m):
        fr, fi = f_hat[l, 0:H, :], f_hat[l, H:N, :]
        dr, di = d_hat[0:H, lanes(m)], d_hat[H:N, lanes(m)]
        d_mix = inverse(jnp.concatenate([fr * dr + fi * di, fr * di - fi * dr], axis=0))
        d_str[1, m, 0:T, :] = rounded(d_mix * value[l, m])
        d_str[2, m, 0:T, :] = rounded(d_mix * key[l, m])
        taps = [[sf[l, i * KS + j] for j in range(KS)] for i in range(3)]

        def normed_chunk(t):
            total = None
            for i in range(3):
                for j in range(KS):
                    term = taps[i][j] * d_str[i, m, pl.ds(t + j, CHUNK), :]
                    total = term if total is None else total + term
            d_nor[m, pl.ds(t, CHUNK), :] = total

        chunks(normed_chunk)

    def long_gradient(l):
        re, im = None, None
        for m in range(M):
            dr, di = d_hat[0:H, lanes(m)], d_hat[H:N, lanes(m)]
            mr, mi = m_hat[l, 0:H, lanes(m)], m_hat[l, H:N, lanes(m)]
            a, b = dr * mr + di * mi, di * mr - dr * mi
            re, im = (a, b) if re is None else (re + a, im + b)
        taps_grad = mm3(iv[0, 0:KL, :], iv[1, 0:KL, :], jnp.concatenate([re, im], axis=0))
        fresh[3 * KS:3 * KS + KL, :] = taps_grad
        fresh[3 * KS + KL:3 * KS + KL + 1, :] = taps_grad[0:1]
        fresh_out[l, early_low:early_high, :] = fresh[early_low:early_high, :].astype(BF16)
        send_rows(l, 0, early_low, early_high)

    def short_gradients(l):
        fold = lambda v: jnp.sum(v.reshape(CHUNK // 8, 8, W), axis=0)
        zeros = tuple(jnp.zeros((8, W), F32) for _ in range(3 * KS + 1))

        def grad_chunk(i, carry):
            t = pl.multiple_of(i * CHUNK, CHUNK)
            sums = list(carry)
            for m in range(M):
                streams = [d_str[k, m, pl.ds(t, CHUNK), :] for k in range(3)]
                for j in range(KS):
                    shifted_rows = normed[l, m, pl.ds(t + PAD - j, CHUNK), :]
                    for k in range(3):
                        sums[k * KS + j] = sums[k * KS + j] + fold(streams[k] * shifted_rows)
                gain_terms = d_nor[m, pl.ds(t, CHUNK), :] * xf[l, m, pl.ds(t, CHUNK), :] * scale[l, m, pl.ds(t, CHUNK), :]
                sums[3 * KS] = sums[3 * KS] + fold(gain_terms)
            return tuple(sums)

        sums = lax.fori_loop(0, T // CHUNK, grad_chunk, zeros)
        for row in range(3 * KS):
            fresh[row:row + 1, :] = jnp.sum(sums[row], axis=0, keepdims=True)
        fresh[rows_total - 1:rows_total, :] = jnp.sum(sums[3 * KS], axis=0, keepdims=True)
        for index in (1, 2):
            low, high = spans[index]
            fresh_out[l, low:high, :] = fresh[low:high, :].astype(BF16)
            send_rows(l, index, low, high)

    for l in range(L - 1):
        for m in range(M):
            if l == 0:
                for copy in x_copies[m]:
                    copy.wait_recv()
                xf[0, m] = x_all[m].astype(F32)
            if l > 0:
                scale[l, m] = as_columns(lax.rsqrt(exchanged(l - 1, m) / D + EPSILON), W)
            forward_and_on(l, m)
    top = L - 1
    for copy in g_copies:
        copy.start()
    for m in range(M):
        scale[top, m] = as_columns(lax.rsqrt(exchanged(top - 1, m) / D + EPSILON), W)
        forward(top, m)
        if m == 0:
            for copy in g_copies:
                copy.wait_recv()
        backward_filtered(top, m)
        backward_normed(top, m)
        exchange(top, m, ng[top] * d_nor[m] * xf[top, m])
    long_gradient(top)
    for l in reversed(range(L)):
        short_gradients(l)
        if l > 0:
            stage = 2 * top - l
            below = l - 1
            for m in range(M):
                term = as_columns(exchanged(stage, m) / D, W)
                r = scale[l, m]
                e_one[below, m] = rounded(cotangent(l, m) + r * ng[l] * d_nor[m] - xf[l, m] * (r * r * r) * term)
                backward_filtered(below, m)
                if m == M - 1:
                    long_gradient(below)
                backward_normed(below, m)
                if below > 0:
                    exchange(stage + 1, m, ng[below] * d_nor[m] * xf[below, m])

    for index, (low, high) in enumerate(spans):
        for slot in range(slots):
            @pl.when(own != slot)
            def _():
                remote(fresh_out.at[0, low:high, :], arrived.at[slot, low:high, :], o_send.at[0, index, 0],
                       o_recv.at[index, slot], at(s, q, c)).wait_recv()
                place(slot, low, high, arrived[slot, low:high, :].astype(F32))
    for l in range(L):
        for seq in range(Q):
            here = jnp.logical_and(s == l, q == seq)

            @pl.when(jnp.logical_not(here))
            def _():
                for index, (low, high) in enumerate(spans):
                    remote(fresh_out.at[l, low:high, :], arrived.at[own, low:high, :], o_send.at[l, index, seq],
                           o_recv.at[index, own], at(l, seq, c)).wait_send()
    for copy in sum(x_copies, []) + g_copies:
        copy.wait_send()

    def p0_sent(offset, carry):
        p0_copy(offset).wait_send()
        return carry

    lax.fori_loop(1, Q * C, p0_sent, 0)
    for stage in range(STAGES * M):
        def sent(offset, carry):
            p, where = peer(offset)
            remote(part_out.at[stage], part.at[stage, me], p_send.at[stage, p], p_recv.at[stage, me], where).wait_send()
            return carry

        lax.fori_loop(1, P_ALL, sent, 0)


def kernel_fits(mesh, args):
    x, sf, lf = args[0], args[2], args[3]
    S, Q = mesh.shape["section"], mesh.shape["seq"]
    width = x.shape[2] // (S * Q)
    rows = Q * x.shape[1]
    return (S == 2 and sf.shape[0] == 1 and width * S * Q == x.shape[2] and width == 128
            and x.shape[1] % CHUNK == 0 and x.shape[0] * x.shape[1] == 128 and sf.shape[2] <= PAD
            and lf.shape[1] % 128 == 0 and lf.shape[1] <= rows)


def by_channels(mesh, x, g, sf, lf, sk, ng):
    S, Q, C = mesh.shape["section"], mesh.shape["seq"], mesh.shape["chan"]
    M, R, channels = x.shape
    KS, KL = sf.shape[2], lf.shape[1]
    W, T, L, G = channels // (S * Q), Q * R, S, S * Q * C
    N = spectrum_size(T, KL)
    fw, iv = spectrum_tables(T, KL)
    rows_total = 3 * KS + KL + 2
    rows_out = -(-rows_total // 16) * 16
    V, dma = pltpu.VMEM, pltpu.SemaphoreType.DMA
    sizes = (S, Q, C, M, R, W, KS, KL, D)
    big = lambda: V((L, M, T, W), F32)
    spans = 3
    stages = 2 * (L - 1)
    pinned = [pltpu.with_memory_space_constraint(a, pltpu.HBM) for a in (x, g, sf.reshape(3 * KS, 1, channels), lf, sk, ng, jnp.asarray(fw), jnp.asarray(iv))]
    result = pl.pallas_call(
        functools.partial(channel_kernel, sizes),
        out_shape=jax.ShapeDtypeStruct((rows_total * S * Q, W), F32),
        in_specs=[pl.BlockSpec(memory_space=pltpu.HBM)] * 8,
        out_specs=pl.BlockSpec(memory_space=pltpu.VMEM),
        scratch_shapes=[
            V((M, R, channels), BF16), V((M, T, W), BF16), V((M, T, W), BF16),
            V((L, 3 * KS, 1, W), F32), V((L, KL, W), F32), V((L, 1, W), F32), V((L, 1, W), F32),
            V(fw.shape, BF16), V(iv.shape, BF16),
            V((1, M * R), F32), V((Q * C, 1, M * R), F32), V((stages * M, 1, T), F32), V((stages * M, G, 1, T), F32),
            big(), big(), V((L, M, PAD + T, W), F32), big(), big(), big(),
            V((T, M * W), BF16), V((L, N, M * W), F32), big(), V((L, N, W), F32),
            V((T, M * W), BF16), V((N, M * W), F32), V((3, M, T + PAD, W), F32), V((M, T, W), F32),
            V((L, M, T, W), F32), V((rows_out, W), F32), V((L, rows_out, W), BF16), V((S * Q, rows_out, W), BF16),
            dma((9,)), dma((M + 1, Q)), dma((M + 1, Q)), dma((4,)), dma((4,)), dma((Q * C,)), dma((Q * C,)),
            dma((stages * M, G)), dma((stages * M, G)), dma((L, spans, Q)), dma((spans, S * Q)),
        ],
        compiler_params=pltpu.CompilerParams(collective_id=0, has_side_effects=True, vmem_limit_bytes=40 * 1024 * 1024),
    )(*pinned)
    return result.reshape(1, rows_total, channels)


def solution(mesh):
    placed = (
        P(None, "seq", "chan"),
        P(None, "seq", "chan"),
        P("section", None, None, "chan"),
        P("section", None, "chan"),
        P("section", "chan"),
        P("section", "chan"),
    )

    def body(*args):
        if kernel_fits(mesh, args):
            return by_channels(mesh, *args)
        return on_device(*args)

    return jax.shard_map(
        body, mesh=mesh, in_specs=placed, out_specs=P("section", None, "chan"), check_vma=False
    )
```
